32 devices in a mesh: wide: 8 (over y, x, core), by: 4 (over z).
Axes of the slice: x: 2, y: 2, z: 4, core: 2. Of those that a mesh axis runs over, the one named last changes fastest.
Arguments:
- tiles: float32 [704, 512, 512], P(('wide', 'by')), may hold values from -6 to 6
- tile_rows: int32 [704], P(('wide', 'by')), may hold values from 0 to 7
- tile_cols: int32 [704], P(('wide', 'by')), may hold values from 0 to 63, as said below
- start_panel: float32 [32768, 64], P('wide'), may hold values from -6 to 6
Outputs:
- panel: float32 [32768, 64], P('wide')
- factor: float32 [64, 64], replicated
The draws below stay inside these ranges and needn't reach their ends.
Inputs may be any that keep to these rules, and one draw needn't show every extreme that they name: `tile_cols`: within one device's 22 tiles, at most 3 have block columns in the block rows of one index of wide, and one index of wide takes exactly 3 of them.
All inputs are finite; a program needn't handle non-finite values.
Results may differ from the reference program's by a relative error of at most 0.0001.
Values sent between devices are 32-bit elements; how exact they have to be, the bound alone decides.
No kernel may reach another device: no remote copies, remote signals or barrier semaphores. Data moves between devices by JAX's collectives and lax.ppermute only.
A program may use at most 192 MiB of HBM per device.

```python
import jax
import jax.numpy as jnp
from jax import lax

BS = 512
K = 64
RB = 8
TPD = 22
ITERS = 2
CAP = 3
NB = 64
NROWS = 32768
TILES = 704
N_WIDE = 8
N_BY = 4


def tile_lists(key):
    dev_count = N_WIDE * N_BY
    slot_count = N_WIDE * CAP
    key_hot, key_shuffle, key_col, key_row = jax.random.split(jax.random.fold_in(key, 7), 4)
    hot_peer = jax.random.randint(key_hot, (dev_count,), 0, N_WIDE)
    shuffled = jax.vmap(lambda subkey: jax.random.permutation(subkey, slot_count))(jax.random.split(key_shuffle, dev_count))
    is_cold = (shuffled // CAP != hot_peer[:, None]).astype(jnp.int32)
    ordering = jnp.argsort(is_cold, axis=1, stable=True)
    chosen = jnp.take_along_axis(shuffled, ordering, axis=1)[:, :TPD]
    peer_index = chosen // CAP
    col_blocks = peer_index * RB + jax.random.randint(key_col, (dev_count, TPD), 0, RB)
    row_blocks = jax.random.randint(key_row, (dev_count, TPD), 0, RB)
    return (row_blocks.reshape(-1).astype(jnp.int32), col_blocks.reshape(-1).astype(jnp.int32))


def draw_tile_rows(key, part):
    return tile_lists(key)[0]


def draw_tile_cols(key, part):
    return tile_lists(key)[1]


def shard_levels(rng, extent, shards, low, top_value):
    loudness = 1.0
    for position, parts in shards:
        heights = jax.random.uniform(jax.random.fold_in(jax.random.fold_in(rng, 6), position), (parts,), jnp.float32, low / len(shards), top_value / len(shards))
        loudness = loudness * jnp.repeat(jnp.exp(heights), extent[position] // parts).reshape((-1,) + (1,) * (len(extent) - 1 - position))
    return loudness


def bell_draw(rng, shape, scale, bound, shards=(), held_as=jnp.bfloat16):
    entries = scale * jax.random.normal(rng, shape, jnp.float32)
    if shards:
        entries = entries * shard_levels(rng, shape, shards, -0.22, 0.18)
    return jnp.clip(entries, -bound, bound).astype(held_as)


def setup_inputs(seed: int = 0) -> dict:
    seeds = jax.random.split(jax.random.key(seed), 5)
    tiles = bell_draw(seeds[0], (TILES, BS, BS), 1.0, 6.0, ((0, 32),), jnp.float32)
    tile_rows = draw_tile_rows(jax.random.fold_in(seeds[4], 71), 0)
    tile_cols = draw_tile_cols(jax.random.fold_in(seeds[4], 71), 0)
    start_panel = bell_draw(seeds[3], (NROWS, K), 1.0, 6.0, ((0, 8),), jnp.float32)
    return {"tiles": tiles, "tile_rows": tile_rows, "tile_cols": tile_cols, "start_panel": start_panel}


def reference(tiles, tile_rows, tile_cols, start_panel):
    dev_count = N_WIDE * N_BY
    grouped = tiles.reshape(dev_count, TPD, BS, BS)
    owner_base = jnp.arange(dev_count, dtype=jnp.int32) // N_BY * RB
    global_rows = (tile_rows.reshape(dev_count, TPD) + owner_base[:, None]).astype(jnp.int32)
    global_cols = tile_cols.reshape(dev_count, TPD).astype(jnp.int32)
    panel = start_panel
    factor = jnp.zeros((K, K), jnp.float32)
    for step in range(ITERS):
        blocks = panel.reshape(NB, BS, K)

        def visit(total, item):
            group, row_ids, col_ids = item
            direct = jnp.einsum('tab,tbk->tak', group, blocks[col_ids], precision=lax.Precision.HIGHEST)
            mirror = jnp.einsum('tba,tbk->tak', group, blocks[row_ids], precision=lax.Precision.HIGHEST)
            total = total.at[row_ids].add(direct).at[col_ids].add(mirror)
            return (total, None)
        image, _ = lax.scan(visit, jnp.zeros((NB, BS, K), jnp.float32), (grouped, global_rows, global_cols))
        image = image.reshape(NROWS, K)
        gram = jnp.dot(image.T, image, precision=lax.Precision.HIGHEST)
        factor = jnp.linalg.cholesky(gram)
        panel = jax.scipy.linalg.solve_triangular(factor, image.T, lower=True).T
    return (panel, factor)
```

```python
import functools

import jax
import jax.numpy as jnp
from jax import lax
from jax.experimental import pallas as pl
from jax.experimental.pallas import tpu as pltpu
from jax.sharding import PartitionSpec as P

ITERS = 2
HIGHEST = lax.Precision.HIGHEST


def split_pair(x):
    high = x.astype(jnp.bfloat16)
    low = (x - high.astype(jnp.float32)).astype(jnp.bfloat16)
    return high, low


def serve_kernel(wide, cap, bs, place_ref, wanted_ref, *refs):
    n_by = len(refs) - wide - 4
    quarters = refs[:n_by]
    panel_out = refs[n_by]
    outs = refs[n_by + 1 : n_by + 1 + wide]
    whole, in_sem, out_sem = refs[n_by + 1 + wide :]
    me, me_by = place_ref[0], place_ref[1]
    quarter = quarters[0].shape[1]
    loads = []
    for j in range(n_by):
        at = pl.multiple_of((me_by ^ j) * quarter, quarter)
        loads.append(
            pltpu.make_async_copy(quarters[j], whole.at[:, pl.ds(at, quarter)], in_sem.at[j])
        )
    for load in loads:
        load.start()
    for load in loads:
        load.wait()
    stores = [pltpu.make_async_copy(whole, panel_out, out_sem.at[wide * cap])]
    for k in range(wide):
        for c in range(cap):
            block = wanted_ref[(me ^ k) * cap + c]
            at = pl.multiple_of(block * bs, bs)
            stores.append(
                pltpu.make_async_copy(
                    whole.at[:, pl.ds(at, bs)],
                    outs[k].at[:, pl.ds(c * bs, bs)],
                    out_sem.at[k * cap + c],
                )
            )
    for store in stores:
        store.start()
    for store in stores:
        store.wait()


def serve(place, wanted, quarters, wide, cap, bs):
    n_by = len(quarters)
    width, quarter = quarters[0].shape
    rows = quarter * n_by
    shape = functools.partial(jax.ShapeDtypeStruct, dtype=jnp.float32)
    any_spec = pl.BlockSpec(memory_space=pl.ANY)
    outs = pl.pallas_call(
        functools.partial(serve_kernel, wide, cap, bs),
        grid_spec=pltpu.PrefetchScalarGridSpec(
            num_scalar_prefetch=2,
            grid=(),
            in_specs=[any_spec] * n_by,
            out_specs=[any_spec] * (wide + 1),
            scratch_shapes=[
                pltpu.VMEM((width, rows), jnp.float32),
                pltpu.SemaphoreType.DMA((n_by,)),
                pltpu.SemaphoreType.DMA((wide * cap + 1,)),
            ],
        ),
        out_shape=[shape((width, rows))] + [shape((width, cap * bs))] * wide,
        name="serve",
    )(place, wanted, *quarters)
    return outs[0], outs[1:]


def tile_products(stacked, tile, transposed):
    width = stacked.shape[0] // 2
    high, low = split_pair(tile)
    dims = (((1,), (1 if transposed else 0,)), ((), ()))
    both = lax.dot_general(stacked, high, dims, preferred_element_type=jnp.float32)
    rest = lax.dot_general(stacked[:width], low, dims, preferred_element_type=jnp.float32)
    return both[:width] + (both[width:] + rest)


def mirror_kernel(wide, cap, place_ref, tile_ref, row_ref, valid_ref, tile, panel, *refs):
    outs = refs[:wide]
    stacked, = refs[wide:]
    bs = tile.shape[1]
    width = panel.shape[0]
    step = pl.program_id(0)
    slot = (place_ref[0] ^ (step // cap)) * cap + step % cap

    @pl.when(step == 0)
    def _():
        for b in range(stacked.shape[0]):
            high, low = split_pair(panel[:, b * bs : (b + 1) * bs])
            stacked[b, :width] = high
            stacked[b, width:] = low

    def put(value):
        for k in range(wide):
            @pl.when(step // cap == k)
            def _():
                at = pl.multiple_of((step % cap) * bs, bs)
                outs[k][:, pl.ds(at, bs)] = value()

    @pl.when(valid_ref[slot] == 1)
    def _():
        result = tile_products(stacked[row_ref[slot]], tile[0], False)
        put(lambda: result)

    @pl.when(valid_ref[slot] == 0)
    def _():
        put(lambda: jnp.zeros((width, bs), jnp.float32))


def mirror(place, slot_tile, slot_row, slot_valid, tiles, panel, wide, cap):
    width, rows = panel.shape
    bs = tiles.shape[1]
    steps = wide * cap

    def tile_map(step, place, slot_tile, slot_row, slot_valid):
        return (slot_tile[(place[0] ^ (step // cap)) * cap + step % cap], 0, 0)

    whole = lambda step, *_: (0, 0)
    return pl.pallas_call(
        functools.partial(mirror_kernel, wide, cap),
        grid_spec=pltpu.PrefetchScalarGridSpec(
            num_scalar_prefetch=4,
            grid=(steps,),
            in_specs=[pl.BlockSpec((1, bs, bs), tile_map), pl.BlockSpec((width, rows), whole)],
            out_specs=[pl.BlockSpec((width, cap * bs), whole)] * wide,
            scratch_shapes=[pltpu.VMEM((rows // bs, 2 * width, bs), jnp.bfloat16)],
        ),
        out_shape=[jax.ShapeDtypeStruct((width, cap * bs), jnp.float32)] * wide,
        compiler_params=pltpu.CompilerParams(vmem_limit_bytes=48 << 20),
        name="mirror",
    )(place, slot_tile, slot_row, slot_valid, tiles, panel)


def direct_kernel(wide, cap, place_ref, tile_ref, row_ref, valid_ref, tile, *refs):
    received = refs[:wide]
    total, stacked = refs[wide:]
    bs = tile.shape[1]
    width = total.shape[0]
    step = pl.program_id(0)
    slot = (place_ref[0] ^ (step // cap)) * cap + step % cap

    @pl.when(step == 0)
    def _():
        total[...] = jnp.zeros_like(total)

    @pl.when(valid_ref[slot] == 1)
    def _():
        for k in range(wide):
            @pl.when(step // cap == k)
            def _():
                high, low = split_pair(received[k][...])
                stacked[:width] = high
                stacked[width:] = low

        at = pl.multiple_of(row_ref[slot] * bs, bs)
        total[:, pl.ds(at, bs)] += tile_products(stacked[...], tile[0], True)


def direct(place, slot_tile, slot_row, slot_valid, tiles, received, rows, wide, cap):
    bs = tiles.shape[1]
    width = received[0].shape[0]
    steps = wide * cap

    def tile_map(step, place, slot_tile, slot_row, slot_valid):
        return (slot_tile[(place[0] ^ (step // cap)) * cap + step % cap], 0, 0)

    def block_map(k, step, *_):
        return (0, jnp.clip(step - k * cap, 0, cap - 1))

    return pl.pallas_call(
        functools.partial(direct_kernel, wide, cap),
        grid_spec=pltpu.PrefetchScalarGridSpec(
            num_scalar_prefetch=4,
            grid=(steps,),
            in_specs=[pl.BlockSpec((1, bs, bs), tile_map)]
            + [pl.BlockSpec((width, bs), functools.partial(block_map, k)) for k in range(wide)],
            out_specs=pl.BlockSpec((width, rows), lambda step, *_: (0, 0)),
            scratch_shapes=[pltpu.VMEM((2 * width, bs), jnp.bfloat16)],
        ),
        out_shape=jax.ShapeDtypeStruct((width, rows), jnp.float32),
        compiler_params=pltpu.CompilerParams(vmem_limit_bytes=48 << 20),
        name="direct",
    )(place, slot_tile, slot_row, slot_valid, tiles, *received)


def gather_kernel(wide, cap, n_by, bs, place_ref, wanted_ref, flag_ref, start, *refs):
    returned = refs[:wide]
    outs = refs[wide : wide + n_by]
    total, = refs[wide + n_by :]
    step = pl.program_id(0)
    slot = (place_ref[0] ^ (step // cap)) * cap + step % cap

    @pl.when(step == 0)
    def _():
        total[...] = start[...]

    @pl.when(flag_ref[slot] == 1)
    def _():
        at = pl.multiple_of(wanted_ref[slot] * bs, bs)
        for k in range(wide):
            @pl.when(step // cap == k)
            def _():
                total[:, pl.ds(at, bs)] += returned[k][...]

    @pl.when(step == wide * cap - 1)
    def _():
        quarter = outs[0].shape[1]
        for j in range(n_by):
            at = pl.multiple_of((place_ref[1] ^ j) * quarter, quarter)
            outs[j][...] = total[:, pl.ds(at, quarter)]


def gather(place, wanted, flag, start, returned, wide, cap, n_by, bs):
    width, rows = start.shape
    quarter = rows // n_by

    def block_map(k, step, *_):
        return (0, jnp.clip(step - k * cap, 0, cap - 1))

    whole = lambda step, *_: (0, 0)
    return pl.pallas_call(
        functools.partial(gather_kernel, wide, cap, n_by, bs),
        grid_spec=pltpu.PrefetchScalarGridSpec(
            num_scalar_prefetch=3,
            grid=(wide * cap,),
            in_specs=[pl.BlockSpec((width, rows), whole)]
            + [pl.BlockSpec((width, bs), functools.partial(block_map, k)) for k in range(wide)],
            out_specs=[pl.BlockSpec((width, quarter), whole)] * n_by,
            scratch_shapes=[pltpu.VMEM((width, rows), jnp.float32)],
        ),
        out_shape=[jax.ShapeDtypeStruct((width, quarter), jnp.float32)] * n_by,
        compiler_params=pltpu.CompilerParams(vmem_limit_bytes=48 << 20),
        name="gather",
    )(place, wanted, flag, start, *returned)


def cholesky_kernel(gram, factor_t, inverse):
    n = gram.shape[0]
    row = lax.broadcasted_iota(jnp.int32, (n, 2 * n), 0)
    lane = lax.broadcasted_iota(jnp.int32, (n, 2 * n), 1)
    eye = (row[:, :n] == lane[:, :n]).astype(jnp.float32)
    work = jnp.concatenate([gram[...], eye], axis=1)
    for j in range(n):
        scale = 1.0 / jnp.sqrt(work[j : j + 1, j : j + 1])
        pivot_row = work[j : j + 1, :] * scale
        column = work[:, j : j + 1] * scale
        work = jnp.where(row == j, pivot_row, jnp.where(row > j, work - column * pivot_row, work))
    upper = row[:, :n] <= lane[:, :n]
    factor_t[...] = jnp.where(upper, work[:, :n], 0.0)
    inverse[...] = jnp.where(row[:, :n] >= lane[:, :n], work[:, n:], 0.0)


def cholesky(gram):
    n = gram.shape[0]
    shape = jax.ShapeDtypeStruct((n, n), jnp.float32)
    factor_t, inverse = pl.pallas_call(cholesky_kernel, out_shape=[shape, shape], name="cholesky")(gram)
    return factor_t.T, inverse


def final_kernel(place_ref, inverse, *refs):
    quarters, out = refs[:-1], refs[-1]
    quarter = quarters[0].shape[1]
    for j in range(len(quarters)):
        at = pl.multiple_of((place_ref[0] ^ j) * quarter, quarter)
        out[:, pl.ds(at, quarter)] = jnp.dot(
            inverse[...], quarters[j][...], precision=HIGHEST, preferred_element_type=jnp.float32
        )


def final(me_by, inverse, quarters):
    width, quarter = quarters[0].shape
    rows = quarter * len(quarters)
    vmem = pl.BlockSpec(memory_space=pltpu.VMEM)
    return pl.pallas_call(
        final_kernel,
        in_specs=[pl.BlockSpec(memory_space=pltpu.SMEM)] + [vmem] * (1 + len(quarters)),
        out_specs=vmem,
        out_shape=jax.ShapeDtypeStruct((width, rows), jnp.float32),
        compiler_params=pltpu.CompilerParams(vmem_limit_bytes=32 << 20),
        name="final",
    )(me_by, inverse, *quarters)


def local(tiles, tile_rows, tile_cols, start_panel):
    wide = lax.axis_size("wide")
    n_by = lax.axis_size("by")
    me = lax.axis_index("wide")
    me_by = lax.axis_index("by")
    tile_count, bs, _ = tiles.shape
    rows, width = start_panel.shape
    block_rows = rows // bs
    cap = max(2, tile_count // wide + 1)
    slots = wide * cap
    i32 = jnp.int32

    def swap(x, axis, size, k):
        return lax.ppermute(x, axis, [(i, i ^ k) for i in range(size)])

    def swap_wide(parts):
        return [parts[0]] + [swap(parts[k], "wide", wide, k) for k in range(1, wide)]

    peer = tile_cols // block_rows
    order = jnp.arange(tile_count, dtype=i32)
    earlier = (order[:, None] > order[None, :]) & (peer[:, None] == peer[None, :])
    rank = jnp.sum(earlier.astype(i32), axis=1)
    match = (peer * cap + rank)[:, None] == jnp.arange(slots, dtype=i32)[None, :]
    pick = lambda v: jnp.sum(jnp.where(match, v[:, None], 0), axis=0)
    slot_tile = pick(order)
    slot_row = pick(tile_rows)
    slot_valid = pick(jnp.ones_like(order))
    request = pick(tile_cols - peer * block_rows + 1)
    incoming = lax.all_to_all(
        request.reshape(wide, cap), "wide", split_axis=0, concat_axis=0, tiled=True
    ).reshape(slots)
    flag = (incoming > 0).astype(i32)
    wanted = jnp.maximum(incoming - 1, 0)
    place = jnp.stack([me, me_by]).astype(i32)

    def product(panel, served):
        received = swap_wide(served)
        mirrored = mirror(place, slot_tile, slot_row, slot_valid, tiles, panel, wide, cap)
        total = direct(place, slot_tile, slot_row, slot_valid, tiles, received, rows, wide, cap)
        returned = swap_wide(mirrored)
        chunks = gather(place, wanted, flag, total, returned, wide, cap, n_by, bs)
        quarter = chunks[0]
        for j in range(1, n_by):
            quarter = quarter + swap(chunks[j], "by", n_by, j)
        return quarter

    def spread(quarter):
        return [quarter] + [swap(quarter, "by", n_by, j) for j in range(1, n_by)]

    def gram_of(quarter):
        gram = jnp.dot(quarter, quarter.T, precision=HIGHEST)
        for axis, size in (("wide", wide), ("by", n_by)):
            k = 1
            while k < size:
                gram = gram + swap(gram, axis, size, k)
                k *= 2
        return gram

    panel_t = start_panel.T
    parts = [
        lax.dynamic_slice_in_dim(panel_t, (me_by ^ j) * (rows // n_by), rows // n_by, axis=1)
        for j in range(n_by)
    ]
    inverse = None
    for step in range(ITERS):
        panel, served = serve(place, wanted, parts, wide, cap, bs)
        quarter = product(panel, served)
        if inverse is not None:
            quarter = jnp.dot(inverse, quarter, precision=HIGHEST)
        parts = spread(quarter)
        factor, inverse = cholesky(gram_of(quarter))
    out = final(place[1:], inverse, parts)
    return (out.T, factor)


def solution(mesh):
    placed = (P(("wide", "by"), None, None), P(("wide", "by")), P(("wide", "by")), P("wide", None))
    return jax.shard_map(
        local, mesh=mesh, in_specs=placed, out_specs=(P("wide", None), P()), check_vma=False
    )
```

```python
import functools

import jax
import jax.numpy as jnp
from jax import lax
from jax.experimental import pallas as pl
from jax.experimental.pallas import tpu as pltpu
from jax.sharding import PartitionSpec as P

ITERS = 2
HALVES = 2
RING = 6
HIGHEST = lax.Precision.HIGHEST
F32 = jnp.float32
SMEM = pl.BlockSpec(memory_space=pltpu.SMEM)
VMEM = pl.BlockSpec(memory_space=pltpu.VMEM)
ANY = pl.BlockSpec(memory_space=pl.ANY)
HBM = pl.BlockSpec(memory_space=pltpu.HBM)


def shape(*dims):
    return jax.ShapeDtypeStruct(dims, F32)


def params(mib):
    return pltpu.CompilerParams(vmem_limit_bytes=mib << 20)


def block(index, size):
    return pl.ds(pl.multiple_of(index * size, size), size)


def split_pair(x):
    high = x.astype(jnp.bfloat16)
    low = (x - high.astype(F32)).astype(jnp.bfloat16)
    return high, low


def load_kernel(tiles, *refs):
    high, low, ring, sems = refs[-4:]
    count, depth = tiles.shape[0], ring.shape[0]

    def copy(t):
        at = lax.rem(t, depth)
        return pltpu.make_async_copy(tiles.at[t], ring.at[at], sems.at[at])

    for t in range(min(depth, count)):
        copy(t).start()

    def step(t, carry):
        copy(t).wait()
        high[t], low[t] = split_pair(ring[lax.rem(t, depth)])

        @pl.when(t + depth < count)
        def _():
            copy(t + depth).start()

        return carry

    lax.fori_loop(0, count, step, 0)


def load(tiles, after=()):
    split = jax.ShapeDtypeStruct(tiles.shape, jnp.bfloat16)
    return pl.pallas_call(
        load_kernel,
        in_specs=[ANY] * (1 + len(after)),
        out_specs=[VMEM] * 2,
        out_shape=[split] * 2,
        scratch_shapes=[
            pltpu.VMEM((RING,) + tiles.shape[1:], F32),
            pltpu.SemaphoreType.DMA((RING,)),
        ],
        compiler_params=params(8),
        name="load",
    )(tiles, *after)


def tile_products(panel, tile, transposed):
    width = panel.shape[0]
    panel_high, panel_low = split_pair(panel)
    stacked = jnp.concatenate([panel_high, panel_low], axis=0)
    dims = (((1,), (1 if transposed else 0,)), ((), ()))
    both = lax.dot_general(stacked, tile[0][...], dims, preferred_element_type=F32)
    rest = lax.dot_general(panel_high, tile[1][...], dims, preferred_element_type=F32)
    return both[:width] + (both[width:] + rest)


def serve_kernel(chips, group, bs, place, wanted, own, sibling, *refs):
    pair, outs = refs[-chips], refs[1 - chips :]
    core = place[1]
    rows = own.shape[1]
    pair[:, block(core, rows)] = own[...]
    pair[:, block(1 - core, rows)] = sibling[...]
    for k in range(1, chips):
        for i in range(group):
            slot = (place[0] ^ k) * group + i
            outs[k - 1][:, i * bs : (i + 1) * bs] = pair[:, block(wanted[slot], bs)]


def serve(place, wanted, own, sibling, chips, group, bs, after=()):
    width, rows = own.shape
    outs = pl.pallas_call(
        functools.partial(serve_kernel, chips, group, bs),
        in_specs=[SMEM, SMEM, VMEM, VMEM] + [ANY] * len(after),
        out_specs=[VMEM] * chips,
        out_shape=[shape(width, 2 * rows)] + [shape(width, group * bs)] * (chips - 1),
        compiler_params=params(6),
        name="serve",
    )(place, wanted, own, sibling, *after)
    return outs[0], outs[1:]


def panel_block(pieces, at):
    return jnp.concatenate([piece[:, at] for piece in pieces], axis=0)


def visit_tiles(ks, group, place, tile_ref, valid_ref, tiles, body):
    def step(s, carry):
        slot = (place[0] ^ (ks[0] + s // group)) * group + s % group

        @pl.when(valid_ref[slot] == 1)
        def _():
            body(slot, [part.at[tile_ref[slot]] for part in tiles])

        return carry

    lax.fori_loop(0, len(ks) * group, step, 0)


def mirror_kernel(chips, group, parts, place, tile_ref, valid_ref, row_ref, high, low, *refs):
    pairs = refs[:parts]
    outs = refs[1 - chips :]
    bs = high.shape[1]
    base = place[1] * (pairs[0].shape[1] // (2 * bs))

    def body(slot, tile):
        panel = panel_block(pairs, block(base + row_ref[slot], bs))
        value = tile_products(panel, tile, False)
        for k in range(1, chips):
            @pl.when(slot // group == place[0] ^ k)
            def _():
                outs[k - 1][:, block(slot % group, bs)] = value

    visit_tiles(range(1, chips), group, place, tile_ref, valid_ref, [high, low], body)


def mirror(place, tables, tiles, pairs, chips, group, after=()):
    half = pairs[0].shape[0]
    bs = tiles[0].shape[1]
    parts = len(pairs)
    return pl.pallas_call(
        functools.partial(mirror_kernel, chips, group, parts),
        in_specs=[SMEM] * 4 + [VMEM] * 2 + [VMEM] * parts + [ANY] * len(after),
        out_specs=[VMEM] * (chips - 1),
        out_shape=[shape(half * parts, group * bs)] * (chips - 1),
        compiler_params=params(6),
        name="mirror",
    )(place, *tables[:3], *tiles, *pairs, *after)


def own_kernel(group, parts, place, tile_ref, valid_ref, row_ref, col_ref, high, low, *refs):
    pairs, total = refs[:parts], refs[-1]
    bs = high.shape[1]
    base = place[1] * (total.shape[1] // (2 * bs))
    total[...] = jnp.zeros_like(total)

    def body(slot, tile):
        row = block(base + row_ref[slot], bs)
        col = block(col_ref[slot], bs)
        total[:, col] += tile_products(panel_block(pairs, row), tile, False)
        total[:, row] += tile_products(panel_block(pairs, col), tile, True)

    visit_tiles(range(1), group, place, tile_ref, valid_ref, [high, low], body)


def own(place, tables, tiles, pairs, group, after=()):
    parts = len(pairs)
    half, rows = pairs[0].shape
    return pl.pallas_call(
        functools.partial(own_kernel, group, parts),
        in_specs=[SMEM] * 5 + [VMEM] * (2 + parts) + [ANY] * len(after),
        out_specs=VMEM,
        out_shape=shape(half * parts, rows),
        compiler_params=params(6),
        name="own",
    )(place, *tables, *tiles, *pairs, *after)


def direct_kernel(chips, group, parts, place, tile_ref, valid_ref, row_ref, high, low, *refs):
    received = refs[: parts * (chips - 1)]
    start = refs[parts * (chips - 1)]
    total, panel = refs[-2:]
    bs = high.shape[1]
    base = place[1] * (total.shape[1] // (2 * bs))
    total[...] = start[...]

    def body(slot, tile):
        for k in range(1, chips):
            @pl.when(slot // group == place[0] ^ k)
            def _():
                source = [received[h * (chips - 1) + k - 1] for h in range(parts)]
                panel[...] = panel_block(source, block(slot % group, bs))

        row = block(base + row_ref[slot], bs)
        total[:, row] += tile_products(panel[...], tile, True)

    visit_tiles(range(1, chips), group, place, tile_ref, valid_ref, [high, low], body)


def direct(place, tables, tiles, start, received, chips, group, after=()):
    parts = len(received)
    arrived = [x for xs in received for x in xs]
    return pl.pallas_call(
        functools.partial(direct_kernel, chips, group, parts),
        in_specs=[SMEM] * 4 + [VMEM] * (3 + len(arrived)) + [ANY] * len(after),
        out_specs=VMEM,
        out_shape=shape(*start.shape),
        scratch_shapes=[pltpu.VMEM((start.shape[0], tiles[0].shape[1]), F32)],
        compiler_params=params(6),
        name="direct",
    )(place, *tables[:3], *tiles, *arrived, start, *after)


def gather_kernel(chips, group, bs, place, wanted, flag, start, *refs):
    returned = refs[: chips - 1]
    own, sibling, total = refs[-3:]
    total[...] = start[...]
    for k in range(1, chips):
        first = (place[0] ^ k) * group

        def step(i, carry):
            @pl.when(flag[first + i] == 1)
            def _():
                total[:, block(wanted[first + i], bs)] += returned[k - 1][:, block(i, bs)]

            return carry

        lax.fori_loop(0, group, step, 0)
    rows = own.shape[1]
    own[...] = total[:, block(place[1], rows)]
    sibling[...] = total[:, block(1 - place[1], rows)]


def gather(place, wanted, flag, start, returned, chips, group, bs, after=()):
    width, rows = start.shape
    return pl.pallas_call(
        functools.partial(gather_kernel, chips, group, bs),
        in_specs=[SMEM] * 3 + [VMEM] * chips + [ANY] * len(after),
        out_specs=[VMEM] * 2,
        out_shape=[shape(width, rows // 2)] * 2,
        scratch_shapes=[pltpu.VMEM((width, rows), F32)],
        compiler_params=params(6),
        name="gather",
    )(place, wanted, flag, start, *returned, *after)


def deal_kernel(place, own, other, *outs):
    half, quarter = outs[0].shape[0], outs[0].shape[1] // 2
    for n, out in enumerate(outs):
        rows = slice(n // 2 * half, (n // 2 + 1) * half)
        for at, j in enumerate(((0, 3), (1, 2))[n % 2]):
            source = block(place[2] ^ j, quarter)
            out[:, at * quarter : (at + 1) * quarter] = own[rows, source] + other[rows, source]


def deal(place, own, other, n_by, parts):
    width, rows = own.shape
    outs = pl.pallas_call(
        deal_kernel,
        in_specs=[SMEM, VMEM, VMEM],
        out_specs=[VMEM] * (parts * 2),
        out_shape=[shape(width // parts, rows // 2)] * (parts * 2),
        compiler_params=params(6),
        name="deal",
    )(place, own, other)
    return [outs[h * 2 : (h + 1) * 2] for h in range(parts)]


def add_kernel(kept, arrived, mine, other):
    quarter = mine.shape[1]
    mine[...] = kept[:, :quarter] + arrived[:, :quarter]
    other[...] = kept[:, quarter:] + arrived[:, quarter:]


def add_pair(kept, arrived):
    half, both = kept.shape
    return pl.pallas_call(
        add_kernel,
        in_specs=[VMEM] * 2,
        out_specs=[VMEM] * 2,
        out_shape=[shape(half, both // 2)] * 2,
        compiler_params=params(6),
        name="add",
    )(kept, arrived)


def total_kernel(mine, arrived, *refs):
    refs[-1][...] = mine[...] + arrived[...]


def total(mine, arrived, after=()):
    return pl.pallas_call(
        total_kernel,
        in_specs=[VMEM] * 2 + [ANY] * len(after),
        out_specs=VMEM,
        out_shape=shape(*mine.shape),
        compiler_params=params(6),
        name="total",
    )(mine, arrived, *after)


def join_kernel(place, mine, across, nearby, *refs):
    out = refs[-1]
    quarter = mine.shape[1]
    out[:, block(place[2], quarter)] = mine[...]
    out[:, block(place[2] ^ 3, quarter)] = across[...]
    out[:, block(place[2] ^ 1, quarter)] = nearby[:, :quarter]
    out[:, block(place[2] ^ 2, quarter)] = nearby[:, quarter:]


def join(place, mine, across, nearby, after=()):
    half, quarter = mine.shape
    return pl.pallas_call(
        join_kernel,
        in_specs=[SMEM] + [VMEM] * 3 + [ANY] * len(after),
        out_specs=VMEM,
        out_shape=shape(half, quarter * 4),
        compiler_params=params(6),
        name="join",
    )(place, mine, across, nearby, *after)


def cholesky_kernel(gram, factor_t, inverse):
    n = gram.shape[0]
    row = lax.broadcasted_iota(jnp.int32, (n, 2 * n), 0)
    lane = lax.broadcasted_iota(jnp.int32, (n, 2 * n), 1)
    eye = (row[:, :n] == lane[:, :n]).astype(F32)
    work = jnp.concatenate([gram[...], eye], axis=1)
    for j in range(n):
        scale = 1.0 / jnp.sqrt(work[j : j + 1, j : j + 1])
        pivot_row = work[j : j + 1, :] * scale
        column = work[:, j : j + 1] * scale
        work = jnp.where(row == j, pivot_row, jnp.where(row > j, work - column * pivot_row, work))
    upper = row[:, :n] <= lane[:, :n]
    factor_t[...] = jnp.where(upper, work[:, :n], 0.0)
    inverse[...] = jnp.where(row[:, :n] >= lane[:, :n], work[:, n:], 0.0)


def cholesky(gram):
    n = gram.shape[0]
    factor_t, inverse = pl.pallas_call(
        cholesky_kernel, out_shape=[shape(n, n)] * 2, compiler_params=params(8), name="cholesky"
    )(gram)
    return factor_t.T, inverse


def final_kernel(inverse, panel, out):
    out[...] = jnp.dot(inverse[...], panel[...], precision=HIGHEST, preferred_element_type=F32)


def final(inverse, panel):
    return pl.pallas_call(
        final_kernel,
        in_specs=[VMEM] * 2,
        out_specs=VMEM,
        out_shape=shape(*panel.shape),
        compiler_params=params(16),
        name="final",
    )(inverse, panel)


def local(tiles, tile_rows, tile_cols, start_panel):
    wide = lax.axis_size("wide")
    n_by = lax.axis_size("by")
    me = lax.axis_index("wide")
    tile_count, bs, _ = tiles.shape
    rows, width = start_panel.shape
    block_rows = rows // bs
    cap = max(2, tile_count // wide + 1)
    chips, group = wide // 2, 2 * cap
    slots = wide * cap
    i32 = jnp.int32

    def swap(x, axis, k):
        size = wide if axis == "wide" else n_by
        return lax.ppermute(x, axis, [(i, i ^ k) for i in range(size)])

    def swap_core(x):
        return swap(x, "wide", 1)

    def swap_chips(parts):
        return [swap(part, "wide", 2 * (k + 1)) for k, part in enumerate(parts)]

    peer = tile_cols // block_rows
    order = jnp.arange(tile_count, dtype=i32)
    earlier = (order[:, None] > order[None, :]) & (peer[:, None] == peer[None, :])
    rank = jnp.sum(earlier.astype(i32), axis=1)
    match = (peer * cap + rank)[:, None] == jnp.arange(slots, dtype=i32)[None, :]
    pick = lambda v: jnp.sum(jnp.where(match, v[:, None], 0), axis=0)
    request = pick(tile_cols % (2 * block_rows) + 1)
    tables = (pick(order), (request > 0).astype(i32), pick(tile_rows), jnp.maximum(request - 1, 0))
    place = jnp.stack([me // 2, me % 2, lax.axis_index("by")]).astype(i32)

    by_chip = request.reshape(chips, group)
    mine = place[0] ^ jnp.arange(chips, dtype=i32)
    xored = by_chip[mine]
    asked = jnp.stack([jnp.zeros((group,), i32)] + swap_chips([xored[k] for k in range(1, chips)]))
    incoming = asked[mine].reshape(slots)
    flag = (incoming > 0).astype(i32)
    wanted = jnp.maximum(incoming - 1, 0)

    halves = range(HALVES)

    def gate(x, *deps):
        return lax.optimization_barrier((x, *deps))[0] if deps else x

    def all_sum(x, axis, masks, *deps):
        level = [x] + [gate(swap(x, axis, mask), *deps) for mask in masks[1:]]
        while len(level) > 1:
            level = [level[i] + level[i + 1] for i in range(0, len(level), 2)]
        return level[0]

    def gram_of(quarters):
        panel = jnp.concatenate(quarters, axis=0)
        return jnp.dot(panel, panel.T, precision=HIGHEST)

    def gram_chips(gram):
        done = 1
        while done < chips:
            step = min(4, chips // done)
            gram = all_sum(gram, "wide", [2 * done * m for m in range(step)])
            done *= step
        return gram

    def serve_half(own, sibling, after=()):
        return serve(place, wanted, own, sibling, chips, group, bs, after)

    def reduce_halves(start, returned, after=()):
        own, other = gather(place, wanted, flag, start, returned, chips, group, bs)
        dealt = deal(place, own, swap_core(other), n_by, HALVES)
        crossing = [add_pair(kept, swap(sent, "by", 1)) for kept, sent in dealt]
        quarters = []
        for mine, other in crossing:
            quarters.append(total(mine, swap(other, "by", 3), after))
            after = [quarters[-1]]
        return quarters

    def spread(quarter):
        across = swap(quarter, "by", 3)
        nearby = swap(jnp.concatenate([quarter, across], axis=1), "by", 1)
        return quarter, across, nearby

    by_all, core_pair = list(range(n_by)), [0, 1]
    panel_t = start_panel.T
    pair, served = serve_half(panel_t, swap_core(panel_t))
    received = [swap_chips(served)]
    tiles = load(tiles, [pair])
    mirrored = mirror(place, tables, tiles, [pair], chips, group)
    start = own(place, tables, tiles, [pair], group, [mirrored[0]])
    start = direct(place, tables, tiles, start, received, chips, group)
    quarters = reduce_halves(start, swap_chips(mirrored))
    spreads = [spread(quarter) for quarter in quarters]
    gram = all_sum(gram_of(quarters), "wide", core_pair)
    pairs, served, last = [], [], [quarters[-1]]
    for h in halves:
        piece = join(place, *spreads[h], last)
        pair, out = serve_half(piece, swap_core(piece), [gram])
        pairs.append(pair)
        served.append(out)
        if h == 0:
            gram = gram_chips(gram)
            last = [out[0], gram]
    received = [swap_chips(out) for out in served]
    mirrored = mirror(place, tables, tiles, pairs, chips, group)
    returned = swap_chips([gate(x, *received[0]) for x in mirrored])
    gram = all_sum(gram, "by", by_all)
    start = own(place, tables, tiles, pairs, group, [mirrored[0], gram])
    factor, inverse = cholesky(gate(gram, start))
    start = direct(place, tables, tiles, start, received, chips, group, [inverse])
    quarters = reduce_halves(start, returned)
    quarter = jnp.dot(inverse, jnp.concatenate(quarters, axis=0), precision=HIGHEST)
    gram = all_sum(gram_of([quarter]), "by", by_all)
    normal = join(place, *spread(gate(quarter, gram)))
    gram = gram_chips(all_sum(gram, "wide", core_pair))
    factor, inverse = cholesky(gram)
    out = final(inverse, normal)
    return (out.T, factor)


def solution(mesh):
    placed = (P(("wide", "by"), None, None), P(("wide", "by")), P(("wide", "by")), P("wide", None))
    return jax.shard_map(
        local, mesh=mesh, in_specs=placed, out_specs=(P("wide", None), P()), check_vma=False
    )
```

```python
import functools

import jax
import jax.numpy as jnp
from jax import lax
from jax.experimental import pallas as pl
from jax.experimental.pallas import tpu as pltpu
from jax.sharding import PartitionSpec as P

ITERS = 2
HALVES = 2
RING = 6
HIGHEST = lax.Precision.HIGHEST
F32 = jnp.float32
SMEM = pl.BlockSpec(memory_space=pltpu.SMEM)
VMEM = pl.BlockSpec(memory_space=pltpu.VMEM)
ANY = pl.BlockSpec(memory_space=pl.ANY)
HBM = pl.BlockSpec(memory_space=pltpu.HBM)


def shape(*dims):
    return jax.ShapeDtypeStruct(dims, F32)


def params(mib):
    return pltpu.CompilerParams(vmem_limit_bytes=mib << 20)


def block(index, size):
    return pl.ds(pl.multiple_of(index * size, size), size)


def split_pair(x):
    high = x.astype(jnp.bfloat16)
    low = (x - high.astype(F32)).astype(jnp.bfloat16)
    return high, low


def load_kernel(tiles, *refs):
    high, low, ring, sems = refs[-4:]
    count, depth = tiles.shape[0], ring.shape[0]

    def copy(t):
        at = lax.rem(t, depth)
        return pltpu.make_async_copy(tiles.at[t], ring.at[at], sems.at[at])

    for t in range(min(depth, count)):
        copy(t).start()

    def step(t, carry):
        copy(t).wait()
        high[t], low[t] = split_pair(ring[lax.rem(t, depth)])

        @pl.when(t + depth < count)
        def _():
            copy(t + depth).start()

        return carry

    lax.fori_loop(0, count, step, 0)


def load(tiles, after=()):
    split = jax.ShapeDtypeStruct(tiles.shape, jnp.bfloat16)
    return pl.pallas_call(
        load_kernel,
        in_specs=[ANY] * (1 + len(after)),
        out_specs=[VMEM] * 2,
        out_shape=[split] * 2,
        scratch_shapes=[
            pltpu.VMEM((RING,) + tiles.shape[1:], F32),
            pltpu.SemaphoreType.DMA((RING,)),
        ],
        compiler_params=params(8),
        name="load",
    )(tiles, *after)


def tile_products(panel, tile, transposed):
    width = panel.shape[0]
    panel_high, panel_low = split_pair(panel)
    stacked = jnp.concatenate([panel_high, panel_low], axis=0)
    dims = (((1,), (1 if transposed else 0,)), ((), ()))
    both = lax.dot_general(stacked, tile[0][...], dims, preferred_element_type=F32)
    rest = lax.dot_general(panel_high, tile[1][...], dims, preferred_element_type=F32)
    return both[:width] + (both[width:] + rest)


def serve_kernel(chips, group, bs, rows, place, wanted, own, sibling, *refs):
    pair, outs = refs[-chips - 1], refs[-chips:-1]
    core = place[1]
    pair[:, block(core, rows)] = own[:, :rows]
    pair[:, block(1 - core, rows)] = sibling[:, :rows]
    rider = own.shape[1] - rows
    if rider:
        refs[-1][...] = own[:, rows:] + sibling[:, rows:]
    else:
        refs[-1][...] = jnp.zeros_like(refs[-1])
    for k in range(1, chips):
        for i in range(group):
            slot = (place[0] ^ k) * group + i
            outs[k - 1][:, i * bs : (i + 1) * bs] = pair[:, block(wanted[slot], bs)]
        if rider:
            outs[k - 1][:, group * bs :] = refs[-1][...]


def serve(place, wanted, own, sibling, rows, chips, group, bs, after=()):
    width = own.shape[0]
    rider = own.shape[1] - rows
    outs = pl.pallas_call(
        functools.partial(serve_kernel, chips, group, bs, rows),
        in_specs=[SMEM, SMEM, VMEM, VMEM] + [ANY] * len(after),
        out_specs=[VMEM] * (chips + 1),
        out_shape=[shape(width, 2 * rows)]
        + [shape(width, group * bs + rider)] * (chips - 1)
        + [shape(width, 128)],
        compiler_params=params(16),
        name="serve",
    )(place, wanted, own, sibling, *after)
    return outs[0], outs[1:-1], outs[-1]


def panel_block(pieces, at):
    return jnp.concatenate([piece[:, at] for piece in pieces], axis=0)


def visit_tiles(ks, group, place, tile_ref, valid_ref, tiles, body):
    def step(s, carry):
        slot = (place[0] ^ (ks[0] + s // group)) * group + s % group

        @pl.when(valid_ref[slot] == 1)
        def _():
            body(slot, [part.at[tile_ref[slot]] for part in tiles])

        return carry

    lax.fori_loop(0, len(ks) * group, step, 0)


def mirror_kernel(chips, group, parts, place, tile_ref, valid_ref, row_ref, high, low, *refs):
    pairs = refs[:parts]
    outs = refs[-HALVES * (chips - 1) :]
    bs = high.shape[1]
    base = place[1] * (pairs[0].shape[1] // (2 * bs))

    def body(slot, tile):
        panel = panel_block(pairs, block(base + row_ref[slot], bs))
        value = tile_products(panel, tile, False)
        for k in range(1, chips):
            @pl.when(slot // group == place[0] ^ k)
            def _():
                half = value.shape[0] // HALVES
                for h in range(HALVES):
                    out = outs[h * (chips - 1) + k - 1]
                    out[:, block(slot % group, bs)] = value[h * half : (h + 1) * half]

    visit_tiles(range(1, chips), group, place, tile_ref, valid_ref, [high, low], body)


def mirror(place, tables, tiles, pairs, chips, group, after=()):
    half = pairs[0].shape[0]
    bs = tiles[0].shape[1]
    parts = len(pairs)
    outs = pl.pallas_call(
        functools.partial(mirror_kernel, chips, group, parts),
        in_specs=[SMEM] * 4 + [VMEM] * 2 + [VMEM] * parts + [ANY] * len(after),
        out_specs=[VMEM] * (HALVES * (chips - 1)),
        out_shape=[shape(half * parts // HALVES, group * bs)] * (HALVES * (chips - 1)),
        compiler_params=params(6),
        name="mirror",
    )(place, *tables[:3], *tiles, *pairs, *after)
    return [outs[h * (chips - 1) : (h + 1) * (chips - 1)] for h in range(HALVES)]


def own_kernel(group, parts, place, tile_ref, valid_ref, row_ref, col_ref, high, low, *refs):
    pairs, total = refs[:parts], refs[-1]
    bs = high.shape[1]
    base = place[1] * (total.shape[1] // (2 * bs))
    total[...] = jnp.zeros_like(total)

    def body(slot, tile):
        row = block(base + row_ref[slot], bs)
        col = block(col_ref[slot], bs)
        total[:, col] += tile_products(panel_block(pairs, row), tile, False)
        total[:, row] += tile_products(panel_block(pairs, col), tile, True)

    visit_tiles(range(1), group, place, tile_ref, valid_ref, [high, low], body)


def own(place, tables, tiles, pairs, group, after=()):
    parts = len(pairs)
    half, rows = pairs[0].shape
    return pl.pallas_call(
        functools.partial(own_kernel, group, parts),
        in_specs=[SMEM] * 5 + [VMEM] * (2 + parts) + [ANY] * len(after),
        out_specs=VMEM,
        out_shape=shape(half * parts, rows),
        compiler_params=params(6),
        name="own",
    )(place, *tables, *tiles, *pairs, *after)


def direct_kernel(chips, group, parts, place, tile_ref, valid_ref, row_ref, high, low, *refs):
    received = refs[: parts * (chips - 1)]
    start = refs[parts * (chips - 1)]
    total, panel = refs[-2:]
    bs = high.shape[1]
    base = place[1] * (total.shape[1] // (2 * bs))
    total[...] = start[...]

    def body(slot, tile):
        for k in range(1, chips):
            @pl.when(slot // group == place[0] ^ k)
            def _():
                source = [received[h * (chips - 1) + k - 1] for h in range(parts)]
                panel[...] = panel_block(source, block(slot % group, bs))

        row = block(base + row_ref[slot], bs)
        total[:, row] += tile_products(panel[...], tile, True)

    visit_tiles(range(1, chips), group, place, tile_ref, valid_ref, [high, low], body)


def direct(place, tables, tiles, start, received, chips, group, after=()):
    parts = len(received)
    arrived = [x for xs in received for x in xs]
    return pl.pallas_call(
        functools.partial(direct_kernel, chips, group, parts),
        in_specs=[SMEM] * 4 + [VMEM] * (3 + len(arrived)) + [ANY] * len(after),
        out_specs=VMEM,
        out_shape=shape(*start.shape),
        scratch_shapes=[pltpu.VMEM((start.shape[0], tiles[0].shape[1]), F32)],
        compiler_params=params(6),
        name="direct",
    )(place, *tables[:3], *tiles, *arrived, start, *after)


def gather_kernel(chips, group, bs, h, place, wanted, flag, start, *refs):
    returned = refs[: chips - 1]
    own, sibling, total = refs[-3:]
    half = total.shape[0]
    total[...] = start[h * half : (h + 1) * half]
    for k in range(1, chips):
        first = (place[0] ^ k) * group

        def step(i, carry):
            @pl.when(flag[first + i] == 1)
            def _():
                total[:, block(wanted[first + i], bs)] += returned[k - 1][:, block(i, bs)]

            return carry

        lax.fori_loop(0, group, step, 0)
    rows = own.shape[1]
    own[...] = total[:, block(place[1], rows)]
    sibling[...] = total[:, block(1 - place[1], rows)]


def gather(place, wanted, flag, start, returned, chips, group, bs, h, after=()):
    half, rows = returned[0].shape[0], start.shape[1]
    return pl.pallas_call(
        functools.partial(gather_kernel, chips, group, bs, h),
        in_specs=[SMEM] * 3 + [VMEM] * chips + [ANY] * len(after),
        out_specs=[VMEM] * 2,
        out_shape=[shape(half, rows // 2)] * 2,
        scratch_shapes=[pltpu.VMEM((half, rows), F32)],
        compiler_params=params(16),
        name="gather",
    )(place, wanted, flag, start, *returned, *after)


def deal_kernel(place, own, other, kept, sent):
    quarter = kept.shape[1] // 2
    for out, pair in ((kept, (0, 3)), (sent, (1, 2))):
        for at, j in enumerate(pair):
            source = block(place[2] ^ j, quarter)
            out[:, at * quarter : (at + 1) * quarter] = own[:, source] + other[:, source]


def deal(place, own, other):
    half, rows = own.shape
    return pl.pallas_call(
        deal_kernel,
        in_specs=[SMEM, VMEM, VMEM],
        out_specs=[VMEM] * 2,
        out_shape=[shape(half, rows // 2)] * 2,
        compiler_params=params(6),
        name="deal",
    )(place, own, other)


def add_kernel(kept, arrived, mine, other):
    quarter = mine.shape[1]
    mine[...] = kept[:, :quarter] + arrived[:, :quarter]
    other[...] = kept[:, quarter:] + arrived[:, quarter:]


def add_pair(kept, arrived):
    half, both = kept.shape
    return pl.pallas_call(
        add_kernel,
        in_specs=[VMEM] * 2,
        out_specs=[VMEM] * 2,
        out_shape=[shape(half, both // 2)] * 2,
        compiler_params=params(6),
        name="add",
    )(kept, arrived)


def total_kernel(mine, arrived, *refs):
    refs[-1][...] = mine[...] + arrived[...]


def total(mine, arrived, after=()):
    return pl.pallas_call(
        total_kernel,
        in_specs=[VMEM] * 2 + [ANY] * len(after),
        out_specs=VMEM,
        out_shape=shape(*mine.shape),
        compiler_params=params(6),
        name="total",
    )(mine, arrived, *after)


def pack_kernel(segments, *refs):
    out = refs[-1]
    at = 0
    for terms in segments:
        values = [refs[n][:, low:high] for n, low, high in terms]
        width = values[0].shape[1]
        out[:, at : at + width] = sum(values[1:], values[0])
        at += width


def pack(*segments):
    arrays, spec = [], []
    for terms in segments:
        spec.append([(len(arrays) + n, low, high) for n, (_, low, high) in enumerate(terms)])
        arrays += [x for x, _, _ in terms]
    widths = [high - low for (_, low, high), *_ in spec]
    return pl.pallas_call(
        functools.partial(pack_kernel, spec),
        in_specs=[VMEM] * len(arrays),
        out_specs=VMEM,
        out_shape=shape(arrays[0].shape[0], sum(widths)),
        compiler_params=params(6),
        name="pack",
    )(*arrays)


def join_kernel(place, mine, across, nearby, *refs):
    out = refs[-1]
    quarter = mine.shape[1]
    out[:, block(place[2], quarter)] = mine[...]
    out[:, block(place[2] ^ 3, quarter)] = across[:, :quarter]
    out[:, block(place[2] ^ 1, quarter)] = nearby[:, :quarter]
    out[:, block(place[2] ^ 2, quarter)] = nearby[:, quarter : 2 * quarter]
    if out.shape[1] > 4 * quarter:
        out[:, 4 * quarter :] = refs[0][...]


def join(place, mine, across, nearby, rider=None, after=()):
    half, quarter = mine.shape
    riders = [] if rider is None else [rider]
    behind = 0 if rider is None else rider.shape[1]
    return pl.pallas_call(
        join_kernel,
        in_specs=[SMEM] + [VMEM] * (3 + len(riders)) + [ANY] * len(after),
        out_specs=VMEM,
        out_shape=shape(half, quarter * 4 + behind),
        compiler_params=params(6),
        name="join",
    )(place, mine, across, nearby, *riders, *after)


def cholesky_kernel(gram, factor_t, inverse):
    n = gram.shape[0]
    row = lax.broadcasted_iota(jnp.int32, (n, 2 * n), 0)
    lane = lax.broadcasted_iota(jnp.int32, (n, 2 * n), 1)
    eye = (row[:, :n] == lane[:, :n]).astype(F32)
    work = jnp.concatenate([gram[...], eye], axis=1)
    for j in range(n):
        scale = 1.0 / jnp.sqrt(work[j : j + 1, j : j + 1])
        pivot_row = work[j : j + 1, :] * scale
        column = work[:, j : j + 1] * scale
        work = jnp.where(row == j, pivot_row, jnp.where(row > j, work - column * pivot_row, work))
    upper = row[:, :n] <= lane[:, :n]
    factor_t[...] = jnp.where(upper, work[:, :n], 0.0)
    inverse[...] = jnp.where(row[:, :n] >= lane[:, :n], work[:, n:], 0.0)


def cholesky(gram):
    n = gram.shape[0]
    factor_t, inverse = pl.pallas_call(
        cholesky_kernel, out_shape=[shape(n, n)] * 2, compiler_params=params(8), name="cholesky"
    )(gram)
    return factor_t.T, inverse


def final_kernel(inverse, *refs):
    out = refs[-1]
    panel = jnp.concatenate([ref[...] for ref in refs[:-1]], axis=0)
    out[...] = jnp.dot(inverse[...], panel, precision=HIGHEST, preferred_element_type=F32)


def final(inverse, pieces):
    return pl.pallas_call(
        final_kernel,
        in_specs=[VMEM] * (1 + len(pieces)),
        out_specs=VMEM,
        out_shape=shape(inverse.shape[0], pieces[0].shape[1]),
        compiler_params=params(16),
        name="final",
    )(inverse, *pieces)


def local(tiles, tile_rows, tile_cols, start_panel):
    wide = lax.axis_size("wide")
    n_by = lax.axis_size("by")
    me = lax.axis_index("wide")
    tile_count, bs, _ = tiles.shape
    rows, width = start_panel.shape
    block_rows = rows // bs
    cap = max(2, tile_count // wide + 1)
    chips, group = wide // 2, 2 * cap
    slots = wide * cap
    i32 = jnp.int32

    def swap(x, axis, k):
        size = wide if axis == "wide" else n_by
        return lax.ppermute(x, axis, [(i, i ^ k) for i in range(size)])

    def swap_core(x):
        return swap(x, "wide", 1)

    def swap_chips(parts):
        return [swap(part, "wide", 2 * (k + 1)) for k, part in enumerate(parts)]

    peer = tile_cols // block_rows
    order = jnp.arange(tile_count, dtype=i32)
    earlier = (order[:, None] > order[None, :]) & (peer[:, None] == peer[None, :])
    rank = jnp.sum(earlier.astype(i32), axis=1)
    match = (peer * cap + rank)[:, None] == jnp.arange(slots, dtype=i32)[None, :]
    pick = lambda v: jnp.sum(jnp.where(match, v[:, None], 0), axis=0)
    request = pick(tile_cols % (2 * block_rows) + 1)
    tables = (pick(order), (request > 0).astype(i32), pick(tile_rows), jnp.maximum(request - 1, 0))
    place = jnp.stack([me // 2, me % 2, lax.axis_index("by")]).astype(i32)

    by_chip = request.reshape(chips, group)
    mine = place[0] ^ jnp.arange(chips, dtype=i32)
    xored = by_chip[mine]
    asked = jnp.stack([jnp.zeros((group,), i32)] + swap_chips([xored[k] for k in range(1, chips)]))
    incoming = asked[mine].reshape(slots)
    flag = (incoming > 0).astype(i32)
    wanted = jnp.maximum(incoming - 1, 0)

    def gate(x, *deps):
        return lax.optimization_barrier((x, *deps))[0] if deps else x

    def all_sum(x, axis, masks, *deps):
        level = [x] + [gate(swap(x, axis, mask), *deps) for mask in masks[1:]]
        while len(level) > 1:
            level = [level[i] + level[i + 1] for i in range(0, len(level), 2)]
        return level[0]

    def gram_of(quarters):
        panel = jnp.concatenate(quarters, axis=0)
        return jnp.dot(panel, panel.T, precision=HIGHEST)

    def gram_chips(gram):
        done = 1
        while done < chips:
            step = min(4, chips // done)
            gram = all_sum(gram, "wide", [2 * done * m for m in range(step)])
            done *= step
        return gram

    def serve_half(own, sibling, after=()):
        return serve(place, wanted, own, sibling, rows, chips, group, bs, after)

    def reduce_half(h, start, returned, after=(), deps=()):
        own, other = gather(place, wanted, flag, start, returned, chips, group, bs, h, after)
        kept, sent = deal(place, own, swap_core(other))
        arrived = swap(gate(sent, *deps), "by", 1)
        mine, other = add_pair(kept, arrived)
        return kept, arrived, mine, swap(other, "by", 3)

    def fold(gram):
        return jnp.concatenate([gram[: width // 2], gram[width // 2 :]], axis=1)

    def unfold(gram):
        return jnp.concatenate([gram[:, :width], gram[:, width:]], axis=0)

    def tree(level):
        while len(level) > 1:
            level = [level[i] + level[i + 1] for i in range(0, len(level), 2)]
        return level[0]

    by_all, core_pair = list(range(n_by)), [0, 1]
    quart = rows // n_by
    panel_t = start_panel.T
    pair, served, _ = serve_half(panel_t, swap_core(panel_t))
    received = [swap_chips(served)]
    tiles = load(tiles, [pair, flag, wanted, *tables])
    mirrored = mirror(place, tables, tiles, [pair], chips, group)
    start = own(place, tables, tiles, [pair], group, [mirrored[0][0]])
    start = direct(place, tables, tiles, start, received, chips, group)
    returned = [swap_chips(x) for x in mirrored]
    kept, first, mine, last = reduce_half(0, start, returned[0])
    _, _, mine_1, last_1 = reduce_half(1, start, returned[1], [first], [first])
    quarters = [total(mine, last)]
    quarters.append(total(mine_1, last_1, [quarters[0]]))
    every, behind = (0, quart), (quart, quart + 2 * width)
    across = swap(quarters[0], "by", 3)
    nearby = swap(pack([(quarters[0], *every)], [(across, *every)]), "by", 1)
    piece = join(place, quarters[0], across, nearby)
    pair, served, _ = serve_half(piece, swap_core(piece))
    pairs, received = [pair], [swap_chips(served)]
    rider = fold(gram_of(quarters))
    across = swap(pack([(quarters[1], *every)], [(rider, 0, 2 * width)]), "by", 3)
    sums = [(rider, 0, 2 * width), (across, *behind)]
    nearby = swap(pack([(quarters[1], *every)], [(across, *every)], sums), "by", 1)
    rider = pack(sums + [(nearby, 2 * quart, 2 * quart + 2 * width)])
    piece = join(place, quarters[1], across, nearby, rider, [piece])
    pair, served, rider = serve_half(piece, swap_core(piece), [pairs[0]])
    pairs.append(pair)
    received.append(swap_chips(served))
    gram = unfold(tree([rider] + [x[:, group * bs :] for x in received[1]]))
    mirrored = mirror(place, tables, tiles, pairs, chips, group)
    returned = [swap_chips([gate(x, received[1][0]) for x in mirrored[0]])]
    returned.append(swap_chips([gate(x, received[1][-1]) for x in mirrored[1]]))
    start = own(place, tables, tiles, pairs, group, [mirrored[0][0]])
    start = direct(place, tables, tiles, start, received, chips, group)
    kept, first, mine, last = reduce_half(0, start, returned[0])
    factor, inverse = cholesky(gate(gram, kept))
    _, _, mine_1, last_1 = reduce_half(1, start, returned[1], [inverse, first], [first])
    quarters = [total(mine, last)]
    across = swap(quarters[0], "by", 3)
    quarters.append(total(mine_1, last_1, [quarters[0]]))
    whole = jnp.concatenate(quarters, axis=0)
    gram_0 = gram_of([jnp.dot(inverse, whole, precision=HIGHEST)])
    gram_1 = all_sum(gram_0, "by", by_all)
    gram_2 = all_sum(gram_1, "wide", core_pair)
    nearby = swap(pack([(quarters[0], *every)], [(gate(across, gram_0), *every)]), "by", 1)
    pieces = [join(place, quarters[0], across, nearby)]
    across = swap(gate(quarters[1], gram_0), "by", 3)
    nearby = swap(pack([(quarters[1], *every)], [(gate(across, gram_1), *every)]), "by", 1)
    pieces.append(join(place, quarters[1], across, nearby))
    factor, inverse_2 = cholesky(gram_chips(gram_2))
    out = final(jnp.dot(inverse_2, inverse, precision=HIGHEST), pieces)
    return (out.T, factor)


def solution(mesh):
    placed = (P(("wide", "by"), None, None), P(("wide", "by")), P(("wide", "by")), P("wide", None))
    return jax.shard_map(
        local, mesh=mesh, in_specs=placed, out_specs=(P("wide", None), P()), check_vma=False
    )
```

```python
import functools

import jax
import jax.numpy as jnp
from jax import lax
from jax.experimental import pallas as pl
from jax.experimental.pallas import tpu as pltpu
from jax.sharding import PartitionSpec as P

ITERS = 2
HALVES = 2
RING = 6
HIGHEST = lax.Precision.HIGHEST
F32 = jnp.float32
SMEM = pl.BlockSpec(memory_space=pltpu.SMEM)
VMEM = pl.BlockSpec(memory_space=pltpu.VMEM)
ANY = pl.BlockSpec(memory_space=pl.ANY)
HBM = pl.BlockSpec(memory_space=pltpu.HBM)


def shape(*dims):
    return jax.ShapeDtypeStruct(dims, F32)


def params(mib):
    return pltpu.CompilerParams(vmem_limit_bytes=mib << 20)


def block(index, size):
    return pl.ds(pl.multiple_of(index * size, size), size)


def split_pair(x):
    high = x.astype(jnp.bfloat16)
    low = (x - high.astype(F32)).astype(jnp.bfloat16)
    return high, low


def load_kernel(tiles, *refs):
    high, low, ring, sems = refs[-4:]
    count, depth = tiles.shape[0], ring.shape[0]

    def copy(t):
        at = lax.rem(t, depth)
        return pltpu.make_async_copy(tiles.at[t], ring.at[at], sems.at[at])

    for t in range(min(depth, count)):
        copy(t).start()

    def step(t, carry):
        copy(t).wait()
        high[t], low[t] = split_pair(ring[lax.rem(t, depth)])

        @pl.when(t + depth < count)
        def _():
            copy(t + depth).start()

        return carry

    lax.fori_loop(0, count, step, 0)


def load(tiles, after=()):
    split = jax.ShapeDtypeStruct(tiles.shape, jnp.bfloat16)
    return pl.pallas_call(
        load_kernel,
        in_specs=[ANY] * (1 + len(after)),
        out_specs=[VMEM] * 2,
        out_shape=[split] * 2,
        scratch_shapes=[
            pltpu.VMEM((RING,) + tiles.shape[1:], F32),
            pltpu.SemaphoreType.DMA((RING,)),
        ],
        compiler_params=params(8),
        name="load",
    )(tiles, *after)


def tile_products(panel, tile, transposed):
    width = panel.shape[0]
    panel_high, panel_low = split_pair(panel)
    stacked = jnp.concatenate([panel_high, panel_low], axis=0)
    dims = (((1,), (1 if transposed else 0,)), ((), ()))
    both = lax.dot_general(stacked, tile[0][...], dims, preferred_element_type=F32)
    rest = lax.dot_general(panel_high, tile[1][...], dims, preferred_element_type=F32)
    return both[:width] + (both[width:] + rest)


def serve_kernel(chips, group, bs, rows, place, wanted, own, sibling, *refs):
    pair, outs = refs[-chips - 1], refs[-chips:-1]
    core = place[1]
    pair[:, block(core, rows)] = own[:, :rows]
    pair[:, block(1 - core, rows)] = sibling[:, :rows]
    rider = own.shape[1] - rows
    if rider:
        refs[-1][...] = own[:, rows:] + sibling[:, rows:]
    else:
        refs[-1][...] = jnp.zeros_like(refs[-1])
    for k in range(1, chips):
        for i in range(group):
            slot = (place[0] ^ k) * group + i
            outs[k - 1][:, i * bs : (i + 1) * bs] = pair[:, block(wanted[slot], bs)]
        if rider:
            outs[k - 1][:, group * bs :] = refs[-1][...]


def serve(place, wanted, own, sibling, rows, chips, group, bs, after=()):
    width = own.shape[0]
    rider = own.shape[1] - rows
    outs = pl.pallas_call(
        functools.partial(serve_kernel, chips, group, bs, rows),
        in_specs=[SMEM, SMEM, VMEM, VMEM] + [ANY] * len(after),
        out_specs=[VMEM] * (chips + 1),
        out_shape=[shape(width, 2 * rows)]
        + [shape(width, group * bs + rider)] * (chips - 1)
        + [shape(width, 128)],
        compiler_params=params(16),
        name="serve",
    )(place, wanted, own, sibling, *after)
    return outs[0], outs[1:-1], outs[-1]


def panel_block(pieces, at):
    return jnp.concatenate([piece[:, at] for piece in pieces], axis=0)


def visit_tiles(ks, group, place, tile_ref, valid_ref, tiles, body):
    def step(s, carry):
        slot = (place[0] ^ (ks[0] + s // group)) * group + s % group

        @pl.when(valid_ref[slot] == 1)
        def _():
            body(slot, [part.at[tile_ref[slot]] for part in tiles])

        return carry

    lax.fori_loop(0, len(ks) * group, step, 0)


def mirror_kernel(chips, group, parts, place, tile_ref, valid_ref, row_ref, high, low, *refs):
    pairs = refs[:parts]
    outs = refs[1 - chips :]
    bs = high.shape[1]
    base = place[1] * (pairs[0].shape[1] // (2 * bs))

    def body(slot, tile):
        panel = panel_block(pairs, block(base + row_ref[slot], bs))
        value = tile_products(panel, tile, False)
        for k in range(1, chips):
            @pl.when(slot // group == place[0] ^ k)
            def _():
                outs[k - 1][:, block(slot % group, bs)] = value

    visit_tiles(range(1, chips), group, place, tile_ref, valid_ref, [high, low], body)


def mirror(place, tables, tiles, pairs, chips, group, after=()):
    half = pairs[0].shape[0]
    bs = tiles[0].shape[1]
    parts = len(pairs)
    return pl.pallas_call(
        functools.partial(mirror_kernel, chips, group, parts),
        in_specs=[SMEM] * 4 + [VMEM] * 2 + [VMEM] * parts + [ANY] * len(after),
        out_specs=[VMEM] * (chips - 1),
        out_shape=[shape(half * parts, group * bs)] * (chips - 1),
        compiler_params=params(6),
        name="mirror",
    )(place, *tables[:3], *tiles, *pairs, *after)


def own_kernel(group, parts, place, tile_ref, valid_ref, row_ref, col_ref, high, low, *refs):
    pairs, total = refs[:parts], refs[-1]
    bs = high.shape[1]
    base = place[1] * (total.shape[1] // (2 * bs))
    total[...] = jnp.zeros_like(total)

    def body(slot, tile):
        row = block(base + row_ref[slot], bs)
        col = block(col_ref[slot], bs)
        total[:, col] += tile_products(panel_block(pairs, row), tile, False)
        total[:, row] += tile_products(panel_block(pairs, col), tile, True)

    visit_tiles(range(1), group, place, tile_ref, valid_ref, [high, low], body)


def own(place, tables, tiles, pairs, group, after=()):
    parts = len(pairs)
    half, rows = pairs[0].shape
    return pl.pallas_call(
        functools.partial(own_kernel, group, parts),
        in_specs=[SMEM] * 5 + [VMEM] * (2 + parts) + [ANY] * len(after),
        out_specs=VMEM,
        out_shape=shape(half * parts, rows),
        compiler_params=params(6),
        name="own",
    )(place, *tables, *tiles, *pairs, *after)


def direct_kernel(chips, group, parts, place, tile_ref, valid_ref, row_ref, high, low, *refs):
    received = refs[: parts * (chips - 1)]
    start = refs[parts * (chips - 1)]
    total, panel = refs[-2:]
    bs = high.shape[1]
    base = place[1] * (total.shape[1] // (2 * bs))
    total[...] = start[...]

    def body(slot, tile):
        for k in range(1, chips):
            @pl.when(slot // group == place[0] ^ k)
            def _():
                source = [received[h * (chips - 1) + k - 1] for h in range(parts)]
                panel[...] = panel_block(source, block(slot % group, bs))

        row = block(base + row_ref[slot], bs)
        total[:, row] += tile_products(panel[...], tile, True)

    visit_tiles(range(1, chips), group, place, tile_ref, valid_ref, [high, low], body)


def direct(place, tables, tiles, start, received, chips, group, after=()):
    parts = len(received)
    arrived = [x for xs in received for x in xs]
    return pl.pallas_call(
        functools.partial(direct_kernel, chips, group, parts),
        in_specs=[SMEM] * 4 + [VMEM] * (3 + len(arrived)) + [ANY] * len(after),
        out_specs=VMEM,
        out_shape=shape(*start.shape),
        scratch_shapes=[pltpu.VMEM((start.shape[0], tiles[0].shape[1]), F32)],
        compiler_params=params(6),
        name="direct",
    )(place, *tables[:3], *tiles, *arrived, start, *after)


def gather_kernel(chips, group, bs, place, wanted, flag, start, *refs):
    returned = refs[: chips - 1]
    own, sibling, total = refs[-3:]
    total[...] = start[...]
    for k in range(1, chips):
        first = (place[0] ^ k) * group

        def step(i, carry):
            @pl.when(flag[first + i] == 1)
            def _():
                total[:, block(wanted[first + i], bs)] += returned[k - 1][:, block(i, bs)]

            return carry

        lax.fori_loop(0, group, step, 0)
    rows = own.shape[1]
    own[...] = total[:, block(place[1], rows)]
    sibling[...] = total[:, block(1 - place[1], rows)]


def gather(place, wanted, flag, start, returned, chips, group, bs):
    width, rows = start.shape
    return pl.pallas_call(
        functools.partial(gather_kernel, chips, group, bs),
        in_specs=[SMEM] * 3 + [VMEM] * chips,
        out_specs=[VMEM] * 2,
        out_shape=[shape(width, rows // 2)] * 2,
        scratch_shapes=[pltpu.VMEM((width, rows), F32)],
        compiler_params=params(16),
        name="gather",
    )(place, wanted, flag, start, *returned)


def deal_kernel(place, own, other, *outs):
    half, quarter = outs[0].shape[0], outs[0].shape[1] // 2
    for n, out in enumerate(outs):
        rows = slice(n // 2 * half, (n // 2 + 1) * half)
        for at, j in enumerate(((0, 3), (1, 2))[n % 2]):
            source = block(place[2] ^ j, quarter)
            out[:, at * quarter : (at + 1) * quarter] = own[rows, source] + other[rows, source]


def deal(place, own, other):
    width, rows = own.shape
    outs = pl.pallas_call(
        deal_kernel,
        in_specs=[SMEM, VMEM, VMEM],
        out_specs=[VMEM] * (HALVES * 2),
        out_shape=[shape(width // HALVES, rows // 2)] * (HALVES * 2),
        compiler_params=params(6),
        name="deal",
    )(place, own, other)
    return [outs[h * 2 : (h + 1) * 2] for h in range(HALVES)]


def add_kernel(kept, arrived, *refs):
    mine, other = refs[-2:]
    quarter = mine.shape[1]
    mine[...] = kept[:, :quarter] + arrived[:, :quarter]
    other[...] = kept[:, quarter:] + arrived[:, quarter:]


def add_pair(kept, arrived, after=()):
    half, both = kept.shape
    return pl.pallas_call(
        add_kernel,
        in_specs=[VMEM] * 2 + [ANY] * len(after),
        out_specs=[VMEM] * 2,
        out_shape=[shape(half, both // 2)] * 2,
        compiler_params=params(6),
        name="add",
    )(kept, arrived, *after)


def total_kernel(mine, arrived, *refs):
    refs[-1][...] = mine[...] + arrived[...]


def total(mine, arrived, after=()):
    return pl.pallas_call(
        total_kernel,
        in_specs=[VMEM] * 2 + [ANY] * len(after),
        out_specs=VMEM,
        out_shape=shape(*mine.shape),
        compiler_params=params(6),
        name="total",
    )(mine, arrived, *after)


def pack_kernel(segments, *refs):
    out = refs[-1]
    at = 0
    for terms in segments:
        values = [refs[n][:, low:high] for n, low, high in terms]
        width = values[0].shape[1]
        out[:, at : at + width] = sum(values[1:], values[0])
        at += width


def pack(*segments):
    arrays, spec = [], []
    for terms in segments:
        spec.append([(len(arrays) + n, low, high) for n, (_, low, high) in enumerate(terms)])
        arrays += [x for x, _, _ in terms]
    widths = [high - low for (_, low, high), *_ in spec]
    return pl.pallas_call(
        functools.partial(pack_kernel, spec),
        in_specs=[VMEM] * len(arrays),
        out_specs=VMEM,
        out_shape=shape(arrays[0].shape[0], sum(widths)),
        compiler_params=params(6),
        name="pack",
    )(*arrays)


def join_kernel(place, mine, across, nearby, *refs):
    out = refs[-1]
    quarter = mine.shape[1]
    out[:, block(place[2], quarter)] = mine[...]
    out[:, block(place[2] ^ 3, quarter)] = across[:, :quarter]
    out[:, block(place[2] ^ 1, quarter)] = nearby[:, :quarter]
    out[:, block(place[2] ^ 2, quarter)] = nearby[:, quarter : 2 * quarter]
    if out.shape[1] > 4 * quarter:
        out[:, 4 * quarter :] = refs[0][...]


def join(place, mine, across, nearby, rider=None, after=()):
    half, quarter = mine.shape
    riders = [] if rider is None else [rider]
    behind = 0 if rider is None else rider.shape[1]
    return pl.pallas_call(
        join_kernel,
        in_specs=[SMEM] + [VMEM] * (3 + len(riders)) + [ANY] * len(after),
        out_specs=VMEM,
        out_shape=shape(half, quarter * 4 + behind),
        compiler_params=params(6),
        name="join",
    )(place, mine, across, nearby, *riders, *after)


def cholesky_kernel(gram, factor_t, inverse):
    n = gram.shape[0]
    row = lax.broadcasted_iota(jnp.int32, (n, 2 * n), 0)
    lane = lax.broadcasted_iota(jnp.int32, (n, 2 * n), 1)
    eye = (row[:, :n] == lane[:, :n]).astype(F32)
    work = jnp.concatenate([gram[...], eye], axis=1)
    for j in range(n):
        scale = 1.0 / jnp.sqrt(work[j : j + 1, j : j + 1])
        pivot_row = work[j : j + 1, :] * scale
        column = work[:, j : j + 1] * scale
        work = jnp.where(row == j, pivot_row, jnp.where(row > j, work - column * pivot_row, work))
    upper = row[:, :n] <= lane[:, :n]
    factor_t[...] = jnp.where(upper, work[:, :n], 0.0)
    inverse[...] = jnp.where(row[:, :n] >= lane[:, :n], work[:, n:], 0.0)


def cholesky(gram):
    n = gram.shape[0]
    factor_t, inverse = pl.pallas_call(
        cholesky_kernel, out_shape=[shape(n, n)] * 2, compiler_params=params(8), name="cholesky"
    )(gram)
    return factor_t.T, inverse


def final_kernel(inverse, *refs):
    out = refs[-1]
    panel = jnp.concatenate([ref[...] for ref in refs[:-1]], axis=0)
    out[...] = jnp.dot(inverse[...], panel, precision=HIGHEST, preferred_element_type=F32)


def final(inverse, pieces):
    return pl.pallas_call(
        final_kernel,
        in_specs=[VMEM] * (1 + len(pieces)),
        out_specs=VMEM,
        out_shape=shape(inverse.shape[0], pieces[0].shape[1]),
        compiler_params=params(16),
        name="final",
    )(inverse, *pieces)


def local(tiles, tile_rows, tile_cols, start_panel):
    wide = lax.axis_size("wide")
    n_by = lax.axis_size("by")
    me = lax.axis_index("wide")
    tile_count, bs, _ = tiles.shape
    rows, width = start_panel.shape
    block_rows = rows // bs
    cap = max(2, tile_count // wide + 1)
    chips, group = wide // 2, 2 * cap
    slots = wide * cap
    i32 = jnp.int32

    def swap(x, axis, k):
        size = wide if axis == "wide" else n_by
        return lax.ppermute(x, axis, [(i, i ^ k) for i in range(size)])

    def swap_core(x):
        return swap(x, "wide", 1)

    def swap_chips(parts):
        return [swap(part, "wide", 2 * (k + 1)) for k, part in enumerate(parts)]

    peer = tile_cols // block_rows
    order = jnp.arange(tile_count, dtype=i32)
    earlier = (order[:, None] > order[None, :]) & (peer[:, None] == peer[None, :])
    rank = jnp.sum(earlier.astype(i32), axis=1)
    match = (peer * cap + rank)[:, None] == jnp.arange(slots, dtype=i32)[None, :]
    pick = lambda v: jnp.sum(jnp.where(match, v[:, None], 0), axis=0)
    request = pick(tile_cols % (2 * block_rows) + 1)
    tables = (pick(order), (request > 0).astype(i32), pick(tile_rows), jnp.maximum(request - 1, 0))
    place = jnp.stack([me // 2, me % 2, lax.axis_index("by")]).astype(i32)

    by_chip = request.reshape(chips, group)
    mine = place[0] ^ jnp.arange(chips, dtype=i32)
    xored = by_chip[mine]
    asked = jnp.stack([jnp.zeros((group,), i32)] + swap_chips([xored[k] for k in range(1, chips)]))
    incoming = asked[mine].reshape(slots)
    flag = (incoming > 0).astype(i32)
    wanted = jnp.maximum(incoming - 1, 0)

    def gate(x, *deps):
        return lax.optimization_barrier((x, *deps))[0] if deps else x

    def all_sum(x, axis, masks, *deps):
        level = [x] + [gate(swap(x, axis, mask), *deps) for mask in masks[1:]]
        while len(level) > 1:
            level = [level[i] + level[i + 1] for i in range(0, len(level), 2)]
        return level[0]

    def gram_of(quarters):
        panel = jnp.concatenate(quarters, axis=0)
        return jnp.dot(panel, panel.T, precision=HIGHEST)

    def gram_chips(gram):
        done = 1
        while done < chips:
            step = min(4, chips // done)
            gram = all_sum(gram, "wide", [2 * done * m for m in range(step)])
            done *= step
        return gram

    def serve_half(own, sibling, after=()):
        return serve(place, wanted, own, sibling, rows, chips, group, bs, after)

    def deal_halves(start, returned):
        own, other = gather(place, wanted, flag, start, returned, chips, group, bs)
        return deal(place, own, swap_core(other))

    def reduce_half(kept, sent, hold=(), after=()):
        mine, other = add_pair(kept, swap(sent, "by", 1), hold)
        return total(mine, swap(other, "by", 3), after)

    def fold(gram):
        return jnp.concatenate([gram[: width // 2], gram[width // 2 :]], axis=1)

    def unfold(gram):
        return jnp.concatenate([gram[:, :width], gram[:, width:]], axis=0)

    def tree(level):
        while len(level) > 1:
            level = [level[i] + level[i + 1] for i in range(0, len(level), 2)]
        return level[0]

    by_all, core_pair = list(range(n_by)), [0, 1]
    quart = rows // n_by
    panel_t = start_panel.T
    pair, served, _ = serve_half(panel_t, swap_core(panel_t))
    received = [swap_chips(served)]
    tiles = load(tiles, [pair, flag, wanted, *tables])
    mirrored = mirror(place, tables, tiles, [pair], chips, group)
    start = own(place, tables, tiles, [pair], group, [mirrored[0]])
    start = direct(place, tables, tiles, start, received, chips, group)
    every, behind = (0, quart), (quart, quart + 2 * width)
    dealt = deal_halves(start, swap_chips(mirrored))
    quarters = [reduce_half(*dealt[0])]
    across = swap(quarters[0], "by", 3)
    quarters.append(reduce_half(*dealt[1], [], [across]))
    nearby = swap(pack([(quarters[0], *every)], [(across, *every)]), "by", 1)
    piece = join(place, quarters[0], across, nearby)
    pair, served, _ = serve_half(piece, swap_core(piece))
    pairs, received = [pair], [swap_chips(served)]
    rider = gate(fold(gram_of(quarters)), served[0])
    across = swap(pack([(quarters[1], *every)], [(rider, 0, 2 * width)]), "by", 3)
    sums = [(rider, 0, 2 * width), (across, *behind)]
    nearby = swap(pack([(quarters[1], *every)], [(across, *every)], sums), "by", 1)
    rider = pack(sums + [(nearby, 2 * quart, 2 * quart + 2 * width)])
    piece = join(place, quarters[1], across, nearby, rider, received[0])
    pair, served, rider = serve_half(piece, swap_core(piece), received[0])
    pairs.append(pair)
    received.append(swap_chips(served))
    gram = unfold(tree([rider] + [x[:, group * bs :] for x in received[1]]))
    mirrored = mirror(place, tables, tiles, pairs, chips, group)
    returned = swap_chips([gate(x, *received[0], *received[1]) for x in mirrored])
    start = own(place, tables, tiles, pairs, group, [mirrored[0]])
    start = direct(place, tables, tiles, start, received, chips, group, returned[:1])
    dealt = deal_halves(start, returned)
    factor, inverse = cholesky(gate(gram, dealt[0][0]))
    quarters = [reduce_half(*dealt[0], [inverse])]
    across = swap(quarters[0], "by", 3)
    quarters.append(reduce_half(*dealt[1]))
    whole = jnp.concatenate(quarters, axis=0)
    gram_0 = gram_of([jnp.dot(inverse, whole, precision=HIGHEST)])
    gram_1 = all_sum(gram_0, "by", by_all)
    gram_2 = all_sum(gram_1, "wide", core_pair)
    nearby = swap(pack([(quarters[0], *every)], [(gate(across, gram_0), *every)]), "by", 1)
    pieces = [join(place, quarters[0], across, nearby)]
    across = swap(gate(quarters[1], gram_0), "by", 3)
    nearby = swap(pack([(quarters[1], *every)], [(gate(across, gram_1), *every)]), "by", 1)
    pieces.append(join(place, quarters[1], across, nearby))
    factor, inverse_2 = cholesky(gram_chips(gram_2))
    out = final(jnp.dot(inverse_2, inverse, precision=HIGHEST), pieces)
    return (out.T, factor)


def solution(mesh):
    placed = (P(("wide", "by"), None, None), P(("wide", "by")), P(("wide", "by")), P("wide", None))
    return jax.shard_map(
        local, mesh=mesh, in_specs=placed, out_specs=(P("wide", None), P()), check_vma=False
    )
```

```python
import functools

import jax
import jax.numpy as jnp
from jax import lax
from jax.experimental import pallas as pl
from jax.experimental.pallas import tpu as pltpu
from jax.sharding import PartitionSpec as P

ITERS = 2
HALVES = 2
RING = 6
HIGHEST = lax.Precision.HIGHEST
F32 = jnp.float32
SMEM = pl.BlockSpec(memory_space=pltpu.SMEM)
VMEM = pl.BlockSpec(memory_space=pltpu.VMEM)
ANY = pl.BlockSpec(memory_space=pl.ANY)
HBM = pl.BlockSpec(memory_space=pltpu.HBM)


def shape(*dims):
    return jax.ShapeDtypeStruct(dims, F32)


def params(mib):
    return pltpu.CompilerParams(vmem_limit_bytes=mib << 20)


def block(index, size):
    return pl.ds(pl.multiple_of(index * size, size), size)


def split_pair(x):
    high = x.astype(jnp.bfloat16)
    low = (x - high.astype(F32)).astype(jnp.bfloat16)
    return high, low


def load_kernel(tiles, *refs):
    high, low, ring, sems = refs[-4:]
    count, depth = tiles.shape[0], ring.shape[0]

    def copy(t):
        at = lax.rem(t, depth)
        return pltpu.make_async_copy(tiles.at[t], ring.at[at], sems.at[at])

    for t in range(min(depth, count)):
        copy(t).start()

    def step(t, carry):
        copy(t).wait()
        high[t], low[t] = split_pair(ring[lax.rem(t, depth)])

        @pl.when(t + depth < count)
        def _():
            copy(t + depth).start()

        return carry

    lax.fori_loop(0, count, step, 0)


def load(tiles, after=()):
    split = jax.ShapeDtypeStruct(tiles.shape, jnp.bfloat16)
    return pl.pallas_call(
        load_kernel,
        in_specs=[ANY] * (1 + len(after)),
        out_specs=[VMEM] * 2,
        out_shape=[split] * 2,
        scratch_shapes=[
            pltpu.VMEM((RING,) + tiles.shape[1:], F32),
            pltpu.SemaphoreType.DMA((RING,)),
        ],
        compiler_params=params(8),
        name="load",
    )(tiles, *after)


def tile_products(panel, tile, transposed):
    width = panel.shape[0]
    panel_high, panel_low = split_pair(panel)
    stacked = jnp.concatenate([panel_high, panel_low], axis=0)
    dims = (((1,), (1 if transposed else 0,)), ((), ()))
    both = lax.dot_general(stacked, tile[0][...], dims, preferred_element_type=F32)
    rest = lax.dot_general(panel_high, tile[1][...], dims, preferred_element_type=F32)
    return both[:width] + (both[width:] + rest)


def serve_kernel(chips, group, bs, rows, place, wanted, own, sibling, *refs):
    pair, outs = refs[-chips - 1], refs[-chips:-1]
    core = place[1]
    pair[:, block(core, rows)] = own[:, :rows]
    pair[:, block(1 - core, rows)] = sibling[:, :rows]
    rider = own.shape[1] - rows
    if rider:
        refs[-1][...] = own[:, rows:] + sibling[:, rows:]
    else:
        refs[-1][...] = jnp.zeros_like(refs[-1])
    for k in range(1, chips):
        for i in range(group):
            slot = (place[0] ^ k) * group + i
            outs[k - 1][:, i * bs : (i + 1) * bs] = pair[:, block(wanted[slot], bs)]
        if rider:
            outs[k - 1][:, group * bs :] = refs[-1][...]


def serve(place, wanted, own, sibling, rows, chips, group, bs, after=()):
    width = own.shape[0]
    rider = own.shape[1] - rows
    outs = pl.pallas_call(
        functools.partial(serve_kernel, chips, group, bs, rows),
        in_specs=[SMEM, SMEM, VMEM, VMEM] + [ANY] * len(after),
        out_specs=[VMEM] * (chips + 1),
        out_shape=[shape(width, 2 * rows)]
        + [shape(width, group * bs + rider)] * (chips - 1)
        + [shape(width, 128)],
        compiler_params=params(16),
        name="serve",
    )(place, wanted, own, sibling, *after)
    return outs[0], outs[1:-1], outs[-1]


def panel_block(pieces, at):
    return jnp.concatenate([piece[:, at] for piece in pieces], axis=0)


def visit_tiles(ks, group, place, tile_ref, valid_ref, tiles, body):
    def step(s, carry):
        slot = (place[0] ^ (ks[0] + s // group)) * group + s % group

        @pl.when(valid_ref[slot] == 1)
        def _():
            body(slot, [part.at[tile_ref[slot]] for part in tiles])

        return carry

    lax.fori_loop(0, len(ks) * group, step, 0)


def mirror_kernel(chips, group, parts, place, tile_ref, valid_ref, row_ref, high, low, *refs):
    pairs = refs[:parts]
    outs = refs[1 - chips :]
    bs = high.shape[1]
    base = place[1] * (pairs[0].shape[1] // (2 * bs))

    def body(slot, tile):
        panel = panel_block(pairs, block(base + row_ref[slot], bs))
        value = tile_products(panel, tile, False)
        for k in range(1, chips):
            @pl.when(slot // group == place[0] ^ k)
            def _():
                outs[k - 1][:, block(slot % group, bs)] = value

    visit_tiles(range(1, chips), group, place, tile_ref, valid_ref, [high, low], body)


def mirror(place, tables, tiles, pairs, chips, group, after=()):
    half = pairs[0].shape[0]
    bs = tiles[0].shape[1]
    parts = len(pairs)
    return pl.pallas_call(
        functools.partial(mirror_kernel, chips, group, parts),
        in_specs=[SMEM] * 4 + [VMEM] * 2 + [VMEM] * parts + [ANY] * len(after),
        out_specs=[VMEM] * (chips - 1),
        out_shape=[shape(half * parts, group * bs)] * (chips - 1),
        compiler_params=params(6),
        name="mirror",
    )(place, *tables[:3], *tiles, *pairs, *after)


def own_kernel(group, parts, place, tile_ref, valid_ref, row_ref, col_ref, high, low, *refs):
    pairs, total = refs[:parts], refs[-1]
    bs = high.shape[1]
    base = place[1] * (total.shape[1] // (2 * bs))
    total[...] = jnp.zeros_like(total)

    def body(slot, tile):
        row = block(base + row_ref[slot], bs)
        col = block(col_ref[slot], bs)
        total[:, col] += tile_products(panel_block(pairs, row), tile, False)
        total[:, row] += tile_products(panel_block(pairs, col), tile, True)

    visit_tiles(range(1), group, place, tile_ref, valid_ref, [high, low], body)


def own(place, tables, tiles, pairs, group, after=()):
    parts = len(pairs)
    half, rows = pairs[0].shape
    return pl.pallas_call(
        functools.partial(own_kernel, group, parts),
        in_specs=[SMEM] * 5 + [VMEM] * (2 + parts) + [ANY] * len(after),
        out_specs=VMEM,
        out_shape=shape(half * parts, rows),
        compiler_params=params(6),
        name="own",
    )(place, *tables, *tiles, *pairs, *after)


def direct_kernel(chips, group, parts, place, tile_ref, valid_ref, row_ref, high, low, *refs):
    received = refs[: parts * (chips - 1)]
    start = refs[parts * (chips - 1)]
    total, panel = refs[-2:]
    bs = high.shape[1]
    base = place[1] * (total.shape[1] // (2 * bs))
    total[...] = start[...]

    def body(slot, tile):
        for k in range(1, chips):
            @pl.when(slot // group == place[0] ^ k)
            def _():
                source = [received[h * (chips - 1) + k - 1] for h in range(parts)]
                panel[...] = panel_block(source, block(slot % group, bs))

        row = block(base + row_ref[slot], bs)
        total[:, row] += tile_products(panel[...], tile, True)

    visit_tiles(range(1, chips), group, place, tile_ref, valid_ref, [high, low], body)


def direct(place, tables, tiles, start, received, chips, group, after=()):
    parts = len(received)
    arrived = [x for xs in received for x in xs]
    return pl.pallas_call(
        functools.partial(direct_kernel, chips, group, parts),
        in_specs=[SMEM] * 4 + [VMEM] * (3 + len(arrived)) + [ANY] * len(after),
        out_specs=VMEM,
        out_shape=shape(*start.shape),
        scratch_shapes=[pltpu.VMEM((start.shape[0], tiles[0].shape[1]), F32)],
        compiler_params=params(6),
        name="direct",
    )(place, *tables[:3], *tiles, *arrived, start, *after)


def gather_kernel(chips, group, bs, place, wanted, flag, start, *refs):
    returned = refs[: chips - 1]
    own, sibling, total = refs[-3:]
    total[...] = start[...]
    for k in range(1, chips):
        first = (place[0] ^ k) * group

        def step(i, carry):
            @pl.when(flag[first + i] == 1)
            def _():
                total[:, block(wanted[first + i], bs)] += returned[k - 1][:, block(i, bs)]

            return carry

        lax.fori_loop(0, group, step, 0)
    rows = own.shape[1]
    own[...] = total[:, block(place[1], rows)]
    sibling[...] = total[:, block(1 - place[1], rows)]


def gather(place, wanted, flag, start, returned, chips, group, bs):
    width, rows = start.shape
    return pl.pallas_call(
        functools.partial(gather_kernel, chips, group, bs),
        in_specs=[SMEM] * 3 + [VMEM] * chips,
        out_specs=[VMEM] * 2,
        out_shape=[shape(width, rows // 2)] * 2,
        scratch_shapes=[pltpu.VMEM((width, rows), F32)],
        compiler_params=params(16),
        name="gather",
    )(place, wanted, flag, start, *returned)


def deal_kernel(place, own, other, *outs):
    half, quarter = outs[0].shape[0], outs[0].shape[1] // 2
    for n, out in enumerate(outs):
        rows = slice(n // 2 * half, (n // 2 + 1) * half)
        for at, j in enumerate(((0, 3), (1, 2))[n % 2]):
            source = block(place[2] ^ j, quarter)
            out[:, at * quarter : (at + 1) * quarter] = own[rows, source] + other[rows, source]


def deal(place, own, other):
    width, rows = own.shape
    outs = pl.pallas_call(
        deal_kernel,
        in_specs=[SMEM, VMEM, VMEM],
        out_specs=[VMEM] * (HALVES * 2),
        out_shape=[shape(width // HALVES, rows // 2)] * (HALVES * 2),
        compiler_params=params(6),
        name="deal",
    )(place, own, other)
    return [outs[h * 2 : (h + 1) * 2] for h in range(HALVES)]


def add_kernel(kept, arrived, *refs):
    mine, other = refs[-2:]
    quarter = mine.shape[1]
    mine[...] = kept[:, :quarter] + arrived[:, :quarter]
    other[...] = kept[:, quarter:] + arrived[:, quarter:]


def add_pair(kept, arrived, after=()):
    half, both = kept.shape
    return pl.pallas_call(
        add_kernel,
        in_specs=[VMEM] * 2 + [ANY] * len(after),
        out_specs=[VMEM] * 2,
        out_shape=[shape(half, both // 2)] * 2,
        compiler_params=params(6),
        name="add",
    )(kept, arrived, *after)


def total_kernel(mine, arrived, *refs):
    refs[-1][...] = mine[...] + arrived[...]


def total(mine, arrived, after=()):
    return pl.pallas_call(
        total_kernel,
        in_specs=[VMEM] * 2 + [ANY] * len(after),
        out_specs=VMEM,
        out_shape=shape(*mine.shape),
        compiler_params=params(6),
        name="total",
    )(mine, arrived, *after)


def pack_kernel(segments, *refs):
    out = refs[-1]
    at = 0
    for terms in segments:
        values = [refs[n][:, low:high] for n, low, high in terms]
        width = values[0].shape[1]
        out[:, at : at + width] = sum(values[1:], values[0])
        at += width


def pack(*segments):
    arrays, spec = [], []
    for terms in segments:
        spec.append([(len(arrays) + n, low, high) for n, (_, low, high) in enumerate(terms)])
        arrays += [x for x, _, _ in terms]
    widths = [high - low for (_, low, high), *_ in spec]
    return pl.pallas_call(
        functools.partial(pack_kernel, spec),
        in_specs=[VMEM] * len(arrays),
        out_specs=VMEM,
        out_shape=shape(arrays[0].shape[0], sum(widths)),
        compiler_params=params(6),
        name="pack",
    )(*arrays)


def join_kernel(place, mine, across, nearby, *refs):
    out = refs[-1]
    quarter = mine.shape[1]
    out[:, block(place[2], quarter)] = mine[...]
    out[:, block(place[2] ^ 3, quarter)] = across[:, :quarter]
    out[:, block(place[2] ^ 1, quarter)] = nearby[:, :quarter]
    out[:, block(place[2] ^ 2, quarter)] = nearby[:, quarter : 2 * quarter]
    if out.shape[1] > 4 * quarter:
        out[:, 4 * quarter :] = refs[0][...]


def join(place, mine, across, nearby, rider=None, after=()):
    half, quarter = mine.shape
    riders = [] if rider is None else [rider]
    behind = 0 if rider is None else rider.shape[1]
    return pl.pallas_call(
        join_kernel,
        in_specs=[SMEM] + [VMEM] * (3 + len(riders)) + [ANY] * len(after),
        out_specs=VMEM,
        out_shape=shape(half, quarter * 4 + behind),
        compiler_params=params(6),
        name="join",
    )(place, mine, across, nearby, *riders, *after)


def cholesky_kernel(gram, factor_t, inverse):
    n = gram.shape[0]
    row = lax.broadcasted_iota(jnp.int32, (n, 2 * n), 0)
    lane = lax.broadcasted_iota(jnp.int32, (n, 2 * n), 1)
    eye = (row[:, :n] == lane[:, :n]).astype(F32)
    work = jnp.concatenate([gram[...], eye], axis=1)
    for j in range(n):
        column = jnp.broadcast_to(work[:, j : j + 1], (n, 2 * n))
        pivot_row = work[j : j + 1, :] * (1.0 / column[j : j + 1, :])
        work = work - jnp.where(row > j, column, 0.0) * pivot_row
    pivots = jnp.sum(jnp.where(row == lane, work, 0.0), axis=1, keepdims=True)
    work = work * (1.0 / jnp.sqrt(pivots))
    factor_t[...] = jnp.where(row[:, :n] <= lane[:, :n], work[:, :n], 0.0)
    inverse[...] = jnp.where(row[:, :n] >= lane[:, :n], work[:, n:], 0.0)


def cholesky(gram):
    n = gram.shape[0]
    factor_t, inverse = pl.pallas_call(
        cholesky_kernel, out_shape=[shape(n, n)] * 2, compiler_params=params(8), name="cholesky"
    )(gram)
    return factor_t.T, inverse


def final_kernel(inverse, *refs):
    out = refs[-1]
    panel = jnp.concatenate([ref[...] for ref in refs[:-1]], axis=0)
    out[...] = jnp.dot(inverse[...], panel, precision=HIGHEST, preferred_element_type=F32)


def final(inverse, pieces):
    return pl.pallas_call(
        final_kernel,
        in_specs=[VMEM] * (1 + len(pieces)),
        out_specs=VMEM,
        out_shape=shape(inverse.shape[0], pieces[0].shape[1]),
        compiler_params=params(16),
        name="final",
    )(inverse, *pieces)


def local(tiles, tile_rows, tile_cols, start_panel):
    wide = lax.axis_size("wide")
    n_by = lax.axis_size("by")
    me = lax.axis_index("wide")
    tile_count, bs, _ = tiles.shape
    rows, width = start_panel.shape
    block_rows = rows // bs
    cap = max(2, tile_count // wide + 1)
    chips, group = wide // 2, 2 * cap
    slots = wide * cap
    i32 = jnp.int32

    def swap(x, axis, k):
        size = wide if axis == "wide" else n_by
        return lax.ppermute(x, axis, [(i, i ^ k) for i in range(size)])

    def swap_core(x):
        return swap(x, "wide", 1)

    def swap_chips(parts):
        return [swap(part, "wide", 2 * (k + 1)) for k, part in enumerate(parts)]

    peer = tile_cols // block_rows
    order = jnp.arange(tile_count, dtype=i32)
    earlier = (order[:, None] > order[None, :]) & (peer[:, None] == peer[None, :])
    rank = jnp.sum(earlier.astype(i32), axis=1)
    match = (peer * cap + rank)[:, None] == jnp.arange(slots, dtype=i32)[None, :]
    pick = lambda v: jnp.sum(jnp.where(match, v[:, None], 0), axis=0)
    request = pick(tile_cols % (2 * block_rows) + 1)
    tables = (pick(order), (request > 0).astype(i32), pick(tile_rows), jnp.maximum(request - 1, 0))
    place = jnp.stack([me // 2, me % 2, lax.axis_index("by")]).astype(i32)

    by_chip = request.reshape(chips, group)
    mine = place[0] ^ jnp.arange(chips, dtype=i32)
    xored = by_chip[mine]
    asked = jnp.stack([jnp.zeros((group,), i32)] + swap_chips([xored[k] for k in range(1, chips)]))
    incoming = asked[mine].reshape(slots)
    flag = (incoming > 0).astype(i32)
    wanted = jnp.maximum(incoming - 1, 0)

    def gate(x, *deps):
        return lax.optimization_barrier((x, *deps))[0] if deps else x

    def all_sum(x, axis, masks, *deps):
        level = [x] + [gate(swap(x, axis, mask), *deps) for mask in masks[1:]]
        while len(level) > 1:
            level = [level[i] + level[i + 1] for i in range(0, len(level), 2)]
        return level[0]

    def gram_of(quarters):
        panel = jnp.concatenate(quarters, axis=0)
        return jnp.dot(panel, panel.T, precision=HIGHEST)

    def gram_chips(gram):
        done = 1
        while done < chips:
            step = min(4, chips // done)
            gram = all_sum(gram, "wide", [2 * done * m for m in range(step)])
            done *= step
        return gram

    def serve_half(own, sibling, after=()):
        return serve(place, wanted, own, sibling, rows, chips, group, bs, after)

    def deal_halves(start, returned):
        own, other = gather(place, wanted, flag, start, returned, chips, group, bs)
        return deal(place, own, swap_core(other))

    def reduce_half(kept, sent, hold=(), after=()):
        mine, other = add_pair(kept, swap(sent, "by", 1), hold)
        return total(mine, swap(other, "by", 3), after)

    def fold(gram):
        return jnp.concatenate([gram[: width // 2], gram[width // 2 :]], axis=1)

    def unfold(gram):
        return jnp.concatenate([gram[:, :width], gram[:, width:]], axis=0)

    def tree(level):
        while len(level) > 1:
            level = [level[i] + level[i + 1] for i in range(0, len(level), 2)]
        return level[0]

    by_all, core_pair = list(range(n_by)), [0, 1]
    quart = rows // n_by
    panel_t = start_panel.T
    pair, served, _ = serve_half(panel_t, swap_core(panel_t))
    received = [swap_chips(served)]
    tiles = load(tiles, [pair, flag, wanted, *tables])
    mirrored = mirror(place, tables, tiles, [pair], chips, group)
    start = own(place, tables, tiles, [pair], group, [mirrored[0]])
    start = direct(place, tables, tiles, start, received, chips, group)
    every, behind = (0, quart), (quart, quart + 2 * width)
    dealt = deal_halves(start, swap_chips(mirrored))
    quarters = [reduce_half(*dealt[0])]
    across = swap(quarters[0], "by", 3)
    quarters.append(reduce_half(*dealt[1], [], [across]))
    nearby = swap(pack([(quarters[0], *every)], [(across, *every)]), "by", 1)
    piece = join(place, quarters[0], across, nearby)
    pair, served, _ = serve_half(piece, swap_core(piece))
    pairs, received = [pair], [swap_chips(served)]
    rider = gate(fold(gram_of(quarters)), served[0])
    across = swap(pack([(quarters[1], *every)], [(rider, 0, 2 * width)]), "by", 3)
    sums = [(rider, 0, 2 * width), (across, *behind)]
    nearby = swap(pack([(quarters[1], *every)], [(across, *every)], sums), "by", 1)
    rider = pack(sums + [(nearby, 2 * quart, 2 * quart + 2 * width)])
    piece = join(place, quarters[1], across, nearby, rider, received[0])
    pair, served, rider = serve_half(piece, swap_core(piece), received[0])
    pairs.append(pair)
    received.append(swap_chips(served))
    gram = unfold(tree([rider] + [x[:, group * bs :] for x in received[1]]))
    mirrored = mirror(place, tables, tiles, pairs, chips, group)
    returned = swap_chips([gate(x, *received[0], *received[1]) for x in mirrored])
    start = own(place, tables, tiles, pairs, group, [mirrored[0]])
    start = direct(place, tables, tiles, start, received, chips, group, returned[:1])
    dealt = deal_halves(start, returned)
    factor, inverse = cholesky(gate(gram, dealt[0][0]))
    quarters = [reduce_half(*dealt[0], [inverse])]
    across = swap(quarters[0], "by", 3)
    quarters.append(reduce_half(*dealt[1]))
    whole = jnp.concatenate(quarters, axis=0)
    gram_0 = gram_of([jnp.dot(inverse, whole, precision=HIGHEST)])
    gram_1 = all_sum(gram_0, "by", by_all)
    gram_2 = all_sum(gram_1, "wide", core_pair)
    nearby = swap(pack([(quarters[0], *every)], [(gate(across, gram_0), *every)]), "by", 1)
    pieces = [join(place, quarters[0], across, nearby)]
    across = swap(gate(quarters[1], gram_0), "by", 3)
    nearby = swap(pack([(quarters[1], *every)], [(gate(across, gram_1), *every)]), "by", 1)
    pieces.append(join(place, quarters[1], across, nearby))
    factor, inverse_2 = cholesky(gram_chips(gram_2))
    out = final(jnp.dot(inverse_2, inverse, precision=HIGHEST), pieces)
    return (out.T, factor)


def solution(mesh):
    placed = (P(("wide", "by"), None, None), P(("wide", "by")), P(("wide", "by")), P("wide", None))
    return jax.shard_map(
        local, mesh=mesh, in_specs=placed, out_specs=(P("wide", None), P()), check_vma=False
    )
```

```python
import functools

import jax
import jax.numpy as jnp
from jax import lax
from jax.experimental import pallas as pl
from jax.experimental.pallas import tpu as pltpu
from jax.sharding import PartitionSpec as P

ITERS = 2
HALVES = 2
RING = 6
HIGHEST = lax.Precision.HIGHEST
F32 = jnp.float32
SMEM = pl.BlockSpec(memory_space=pltpu.SMEM)
VMEM = pl.BlockSpec(memory_space=pltpu.VMEM)
ANY = pl.BlockSpec(memory_space=pl.ANY)
HBM = pl.BlockSpec(memory_space=pltpu.HBM)


def shape(*dims):
    return jax.ShapeDtypeStruct(dims, F32)


def params(mib):
    return pltpu.CompilerParams(vmem_limit_bytes=mib << 20)


def block(index, size):
    return pl.ds(pl.multiple_of(index * size, size), size)


def split_pair(x):
    high = x.astype(jnp.bfloat16)
    low = (x - high.astype(F32)).astype(jnp.bfloat16)
    return high, low


def load_kernel(tiles, *refs):
    high, low, ring, sems = refs[-4:]
    count, depth = tiles.shape[0], ring.shape[0]

    def copy(t):
        at = lax.rem(t, depth)
        return pltpu.make_async_copy(tiles.at[t], ring.at[at], sems.at[at])

    for t in range(min(depth, count)):
        copy(t).start()

    def step(t, carry):
        copy(t).wait()
        high[t], low[t] = split_pair(ring[lax.rem(t, depth)])

        @pl.when(t + depth < count)
        def _():
            copy(t + depth).start()

        return carry

    lax.fori_loop(0, count, step, 0)


def load(tiles, after=()):
    split = jax.ShapeDtypeStruct(tiles.shape, jnp.bfloat16)
    return pl.pallas_call(
        load_kernel,
        in_specs=[ANY] * (1 + len(after)),
        out_specs=[VMEM] * 2,
        out_shape=[split] * 2,
        scratch_shapes=[
            pltpu.VMEM((RING,) + tiles.shape[1:], F32),
            pltpu.SemaphoreType.DMA((RING,)),
        ],
        compiler_params=params(8),
        name="load",
    )(tiles, *after)


def tile_products(panel, tile, transposed):
    width = panel.shape[0]
    panel_high, panel_low = split_pair(panel)
    stacked = jnp.concatenate([panel_high, panel_low], axis=0)
    dims = (((1,), (1 if transposed else 0,)), ((), ()))
    both = lax.dot_general(stacked, tile[0][...], dims, preferred_element_type=F32)
    rest = lax.dot_general(panel_high, tile[1][...], dims, preferred_element_type=F32)
    return both[:width] + (both[width:] + rest)


def serve_kernel(chips, group, bs, rows, place, wanted, own, sibling, *refs):
    pair, outs = refs[-chips - 1], refs[-chips:-1]
    core = place[1]
    pair[:, block(core, rows)] = own[:, :rows]
    pair[:, block(1 - core, rows)] = sibling[:, :rows]
    rider = own.shape[1] - rows
    if rider:
        refs[-1][...] = own[:, rows:] + sibling[:, rows:]
    else:
        refs[-1][...] = jnp.zeros_like(refs[-1])
    for k in range(1, chips):
        for i in range(group):
            slot = (place[0] ^ k) * group + i
            outs[k - 1][:, i * bs : (i + 1) * bs] = pair[:, block(wanted[slot], bs)]
        if rider:
            outs[k - 1][:, group * bs :] = refs[-1][...]


def serve(place, wanted, own, sibling, rows, chips, group, bs, after=()):
    width = own.shape[0]
    rider = own.shape[1] - rows
    outs = pl.pallas_call(
        functools.partial(serve_kernel, chips, group, bs, rows),
        in_specs=[SMEM, SMEM, VMEM, VMEM] + [ANY] * len(after),
        out_specs=[VMEM] * (chips + 1),
        out_shape=[shape(width, 2 * rows)]
        + [shape(width, group * bs + rider)] * (chips - 1)
        + [shape(width, 128)],
        compiler_params=params(16),
        name="serve",
    )(place, wanted, own, sibling, *after)
    return outs[0], outs[1:-1], outs[-1]


def panel_block(pieces, at):
    return jnp.concatenate([piece[:, at] for piece in pieces], axis=0)


def visit_tiles(ks, group, place, tile_ref, valid_ref, tiles, body):
    def step(s, carry):
        slot = (place[0] ^ (ks[0] + s // group)) * group + s % group

        @pl.when(valid_ref[slot] == 1)
        def _():
            body(slot, [part.at[tile_ref[slot]] for part in tiles])

        return carry

    lax.fori_loop(0, len(ks) * group, step, 0)


def mirror_kernel(chips, group, parts, place, tile_ref, valid_ref, row_ref, high, low, *refs):
    pairs = refs[:parts]
    outs = refs[1 - chips :]
    bs = high.shape[1]
    base = place[1] * (pairs[0].shape[1] // (2 * bs))

    def body(slot, tile):
        panel = panel_block(pairs, block(base + row_ref[slot], bs))
        value = tile_products(panel, tile, False)
        for k in range(1, chips):
            @pl.when(slot // group == place[0] ^ k)
            def _():
                outs[k - 1][:, block(slot % group, bs)] = value

    visit_tiles(range(1, chips), group, place, tile_ref, valid_ref, [high, low], body)


def mirror(place, tables, tiles, pairs, chips, group, after=()):
    half = pairs[0].shape[0]
    bs = tiles[0].shape[1]
    parts = len(pairs)
    return pl.pallas_call(
        functools.partial(mirror_kernel, chips, group, parts),
        in_specs=[SMEM] * 4 + [VMEM] * 2 + [VMEM] * parts + [ANY] * len(after),
        out_specs=[VMEM] * (chips - 1),
        out_shape=[shape(half * parts, group * bs)] * (chips - 1),
        compiler_params=params(6),
        name="mirror",
    )(place, *tables[:3], *tiles, *pairs, *after)


def own_kernel(group, parts, place, tile_ref, valid_ref, row_ref, col_ref, high, low, *refs):
    pairs, total = refs[:parts], refs[-1]
    bs = high.shape[1]
    base = place[1] * (total.shape[1] // (2 * bs))
    total[...] = jnp.zeros_like(total)

    def body(slot, tile):
        row = block(base + row_ref[slot], bs)
        col = block(col_ref[slot], bs)
        total[:, col] += tile_products(panel_block(pairs, row), tile, False)
        total[:, row] += tile_products(panel_block(pairs, col), tile, True)

    visit_tiles(range(1), group, place, tile_ref, valid_ref, [high, low], body)


def own(place, tables, tiles, pairs, group, after=()):
    parts = len(pairs)
    half, rows = pairs[0].shape
    return pl.pallas_call(
        functools.partial(own_kernel, group, parts),
        in_specs=[SMEM] * 5 + [VMEM] * (2 + parts) + [ANY] * len(after),
        out_specs=VMEM,
        out_shape=shape(half * parts, rows),
        compiler_params=params(6),
        name="own",
    )(place, *tables, *tiles, *pairs, *after)


def direct_kernel(chips, group, parts, place, tile_ref, valid_ref, row_ref, high, low, *refs):
    received = refs[: parts * (chips - 1)]
    start = refs[parts * (chips - 1)]
    total, panel = refs[-2:]
    bs = high.shape[1]
    base = place[1] * (total.shape[1] // (2 * bs))
    total[...] = start[...]

    def body(slot, tile):
        for k in range(1, chips):
            @pl.when(slot // group == place[0] ^ k)
            def _():
                source = [received[h * (chips - 1) + k - 1] for h in range(parts)]
                panel[...] = panel_block(source, block(slot % group, bs))

        row = block(base + row_ref[slot], bs)
        total[:, row] += tile_products(panel[...], tile, True)

    visit_tiles(range(1, chips), group, place, tile_ref, valid_ref, [high, low], body)


def direct(place, tables, tiles, start, received, chips, group, after=()):
    parts = len(received)
    arrived = [x for xs in received for x in xs]
    return pl.pallas_call(
        functools.partial(direct_kernel, chips, group, parts),
        in_specs=[SMEM] * 4 + [VMEM] * (3 + len(arrived)) + [ANY] * len(after),
        out_specs=VMEM,
        out_shape=shape(*start.shape),
        scratch_shapes=[pltpu.VMEM((start.shape[0], tiles[0].shape[1]), F32)],
        compiler_params=params(6),
        name="direct",
    )(place, *tables[:3], *tiles, *arrived, start, *after)


def gather_kernel(chips, group, bs, place, wanted, flag, start, *refs):
    returned = refs[: chips - 1]
    own, sibling, total = refs[-3:]
    total[...] = start[...]
    for k in range(1, chips):
        first = (place[0] ^ k) * group

        def step(i, carry):
            @pl.when(flag[first + i] == 1)
            def _():
                total[:, block(wanted[first + i], bs)] += returned[k - 1][:, block(i, bs)]

            return carry

        lax.fori_loop(0, group, step, 0)
    rows = own.shape[1]
    own[...] = total[:, block(place[1], rows)]
    sibling[...] = total[:, block(1 - place[1], rows)]


def gather(place, wanted, flag, start, returned, chips, group, bs):
    width, rows = start.shape
    return pl.pallas_call(
        functools.partial(gather_kernel, chips, group, bs),
        in_specs=[SMEM] * 3 + [VMEM] * chips,
        out_specs=[VMEM] * 2,
        out_shape=[shape(width, rows // 2)] * 2,
        scratch_shapes=[pltpu.VMEM((width, rows), F32)],
        compiler_params=params(16),
        name="gather",
    )(place, wanted, flag, start, *returned)


def deal_kernel(place, own, other, *outs):
    half, quarter = outs[0].shape[0], outs[0].shape[1] // 2
    for n, out in enumerate(outs):
        rows = slice(n // 2 * half, (n // 2 + 1) * half)
        for at, j in enumerate(((0, 3), (1, 2))[n % 2]):
            source = block(place[2] ^ j, quarter)
            out[:, at * quarter : (at + 1) * quarter] = own[rows, source] + other[rows, source]


def deal(place, own, other):
    width, rows = own.shape
    outs = pl.pallas_call(
        deal_kernel,
        in_specs=[SMEM, VMEM, VMEM],
        out_specs=[VMEM] * (HALVES * 2),
        out_shape=[shape(width // HALVES, rows // 2)] * (HALVES * 2),
        compiler_params=params(6),
        name="deal",
    )(place, own, other)
    return [outs[h * 2 : (h + 1) * 2] for h in range(HALVES)]


def add_kernel(kept, arrived, *refs):
    mine, other = refs[-2:]
    quarter = mine.shape[1]
    mine[...] = kept[:, :quarter] + arrived[:, :quarter]
    other[...] = kept[:, quarter:] + arrived[:, quarter:]


def add_pair(kept, arrived, after=()):
    half, both = kept.shape
    return pl.pallas_call(
        add_kernel,
        in_specs=[VMEM] * 2 + [ANY] * len(after),
        out_specs=[VMEM] * 2,
        out_shape=[shape(half, both // 2)] * 2,
        compiler_params=params(6),
        name="add",
    )(kept, arrived, *after)


def total_kernel(mine, arrived, *refs):
    refs[-1][...] = mine[...] + arrived[...]


def total(mine, arrived, after=()):
    return pl.pallas_call(
        total_kernel,
        in_specs=[VMEM] * 2 + [ANY] * len(after),
        out_specs=VMEM,
        out_shape=shape(*mine.shape),
        compiler_params=params(6),
        name="total",
    )(mine, arrived, *after)


def pack_kernel(segments, *refs):
    out = refs[-1]
    at = 0
    for terms in segments:
        values = [refs[n][:, low:high] for n, low, high in terms]
        width = values[0].shape[1]
        out[:, at : at + width] = sum(values[1:], values[0])
        at += width


def pack(*segments):
    arrays, spec = [], []
    for terms in segments:
        spec.append([(len(arrays) + n, low, high) for n, (_, low, high) in enumerate(terms)])
        arrays += [x for x, _, _ in terms]
    widths = [high - low for (_, low, high), *_ in spec]
    return pl.pallas_call(
        functools.partial(pack_kernel, spec),
        in_specs=[VMEM] * len(arrays),
        out_specs=VMEM,
        out_shape=shape(arrays[0].shape[0], sum(widths)),
        compiler_params=params(6),
        name="pack",
    )(*arrays)


def join_kernel(place, mine, across, nearby, *refs):
    out = refs[-1]
    quarter = mine.shape[1]
    out[:, block(place[2], quarter)] = mine[...]
    out[:, block(place[2] ^ 3, quarter)] = across[:, :quarter]
    out[:, block(place[2] ^ 1, quarter)] = nearby[:, :quarter]
    out[:, block(place[2] ^ 2, quarter)] = nearby[:, quarter : 2 * quarter]
    if out.shape[1] > 4 * quarter:
        out[:, 4 * quarter :] = refs[0][...]


def join(place, mine, across, nearby, rider=None, after=()):
    half, quarter = mine.shape
    riders = [] if rider is None else [rider]
    behind = 0 if rider is None else rider.shape[1]
    return pl.pallas_call(
        join_kernel,
        in_specs=[SMEM] + [VMEM] * (3 + len(riders)) + [ANY] * len(after),
        out_specs=VMEM,
        out_shape=shape(half, quarter * 4 + behind),
        compiler_params=params(6),
        name="join",
    )(place, mine, across, nearby, *riders, *after)


def cholesky_kernel(gram, factor_t, inverse):
    n = gram.shape[0]
    row = lax.broadcasted_iota(jnp.int32, (n, 2 * n), 0)
    lane = lax.broadcasted_iota(jnp.int32, (n, 2 * n), 1)
    eye = (row[:, :n] == lane[:, :n]).astype(F32)
    work = jnp.concatenate([gram[...], eye], axis=1)
    for j in range(n):
        column = jnp.broadcast_to(work[:, j : j + 1], (n, 2 * n))
        pivot_row = work[j : j + 1, :] * (1.0 / column[j : j + 1, :])
        work = work - jnp.where(row > j, column, 0.0) * pivot_row
    pivots = jnp.sum(jnp.where(row == lane, work, 0.0), axis=1, keepdims=True)
    work = work * (1.0 / jnp.sqrt(pivots))
    factor_t[...] = jnp.where(row[:, :n] <= lane[:, :n], work[:, :n], 0.0)
    inverse[...] = jnp.where(row[:, :n] >= lane[:, :n], work[:, n:], 0.0)


def cholesky(gram):
    n = gram.shape[0]
    factor_t, inverse = pl.pallas_call(
        cholesky_kernel, out_shape=[shape(n, n)] * 2, compiler_params=params(8), name="cholesky"
    )(gram)
    return factor_t.T, inverse


def final_kernel(inverse, *refs):
    out = refs[-1]
    panel = jnp.concatenate([ref[...] for ref in refs[:-1]], axis=0)
    out[...] = jnp.dot(inverse[...], panel, precision=HIGHEST, preferred_element_type=F32)


def final(inverse, pieces):
    return pl.pallas_call(
        final_kernel,
        in_specs=[VMEM] * (1 + len(pieces)),
        out_specs=VMEM,
        out_shape=shape(inverse.shape[0], pieces[0].shape[1]),
        compiler_params=params(16),
        name="final",
    )(inverse, *pieces)


def local(tiles, tile_rows, tile_cols, start_panel):
    wide = lax.axis_size("wide")
    n_by = lax.axis_size("by")
    me = lax.axis_index("wide")
    tile_count, bs, _ = tiles.shape
    rows, width = start_panel.shape
    block_rows = rows // bs
    cap = max(2, tile_count // wide + 1)
    chips, group = wide // 2, 2 * cap
    slots = wide * cap
    i32 = jnp.int32

    def swap(x, axis, k):
        size = wide if axis == "wide" else n_by
        return lax.ppermute(x, axis, [(i, i ^ k) for i in range(size)])

    def swap_core(x):
        return swap(x, "wide", 1)

    def swap_chips(parts):
        return [swap(part, "wide", 2 * (k + 1)) for k, part in enumerate(parts)]

    peer = tile_cols // block_rows
    order = jnp.arange(tile_count, dtype=i32)
    earlier = (order[:, None] > order[None, :]) & (peer[:, None] == peer[None, :])
    rank = jnp.sum(earlier.astype(i32), axis=1)
    match = (peer * cap + rank)[:, None] == jnp.arange(slots, dtype=i32)[None, :]
    pick = lambda v: jnp.sum(jnp.where(match, v[:, None], 0), axis=0)
    request = pick(tile_cols % (2 * block_rows) + 1)
    tables = (pick(order), (request > 0).astype(i32), pick(tile_rows), jnp.maximum(request - 1, 0))
    place = jnp.stack([me // 2, me % 2, lax.axis_index("by")]).astype(i32)

    by_chip = request.reshape(chips, group)
    mine = place[0] ^ jnp.arange(chips, dtype=i32)
    xored = by_chip[mine]
    asked = jnp.stack([jnp.zeros((group,), i32)] + swap_chips([xored[k] for k in range(1, chips)]))
    incoming = asked[mine].reshape(slots)
    flag = (incoming > 0).astype(i32)
    wanted = jnp.maximum(incoming - 1, 0)

    def gate(x, *deps):
        return lax.optimization_barrier((x, *deps))[0] if deps else x

    def all_sum(x, axis, masks, *deps):
        level = [x] + [gate(swap(x, axis, mask), *deps) for mask in masks[1:]]
        while len(level) > 1:
            level = [level[i] + level[i + 1] for i in range(0, len(level), 2)]
        return level[0]

    def gram_of(quarters):
        panel = jnp.concatenate(quarters, axis=0)
        return jnp.dot(panel, panel.T, precision=HIGHEST)

    def gram_chips(gram):
        done = 1
        while done < chips:
            step = min(4, chips // done)
            gram = all_sum(gram, "wide", [2 * done * m for m in range(step)])
            done *= step
        return gram

    def serve_half(own, sibling, after=()):
        return serve(place, wanted, own, sibling, rows, chips, group, bs, after)

    def deal_halves(start, returned):
        own, other = gather(place, wanted, flag, start, returned, chips, group, bs)
        return deal(place, own, swap_core(other))

    def reduce_half(kept, sent, hold=(), after=()):
        mine, other = add_pair(kept, swap(sent, "by", 1), hold)
        return total(mine, swap(other, "by", 3), after)

    def fold(gram):
        return jnp.concatenate([gram[: width // 2], gram[width // 2 :]], axis=1)

    def unfold(gram):
        return jnp.concatenate([gram[:, :width], gram[:, width:]], axis=0)

    def tree(level):
        while len(level) > 1:
            level = [level[i] + level[i + 1] for i in range(0, len(level), 2)]
        return level[0]

    by_all, core_pair = list(range(n_by)), [0, 1]
    quart = rows // n_by
    panel_t = start_panel.T
    pair, served, _ = serve_half(panel_t, swap_core(panel_t))
    received = [swap_chips(served)]
    tiles = load(tiles, [pair, flag, wanted, *tables])
    mirrored = mirror(place, tables, tiles, [pair], chips, group)
    start = own(place, tables, tiles, [pair], group, [mirrored[0]])
    start = direct(place, tables, tiles, start, received, chips, group)
    every, behind = (0, quart), (quart, quart + 2 * width)
    dealt = deal_halves(start, swap_chips(mirrored))
    quarters = [reduce_half(*dealt[0])]
    across = swap(quarters[0], "by", 3)
    quarters.append(reduce_half(*dealt[1], [], [across]))
    nearby = swap(pack([(quarters[0], *every)], [(across, *every)]), "by", 1)
    piece = join(place, quarters[0], across, nearby)
    pair, served, _ = serve_half(piece, swap_core(piece))
    pairs, received = [pair], [swap_chips(served)]
    rider = gate(fold(gram_of(quarters)), served[0])
    across = swap(pack([(quarters[1], *every)], [(rider, 0, 2 * width)]), "by", 3)
    sums = [(rider, 0, 2 * width), (across, *behind)]
    nearby = swap(pack([(quarters[1], *every)], [(across, *every)], sums), "by", 1)
    rider = pack(sums + [(nearby, 2 * quart, 2 * quart + 2 * width)])
    piece = join(place, quarters[1], across, nearby, rider, received[0])
    pair, served, rider = serve_half(piece, swap_core(piece), received[0])
    pairs.append(pair)
    received.append(swap_chips(served))
    gram = unfold(tree([rider] + [x[:, group * bs :] for x in received[1]]))
    mirrored = mirror(place, tables, tiles, pairs, chips, group)
    returned = swap_chips([gate(x, *received[0], *received[1]) for x in mirrored])
    start = own(place, tables, tiles, pairs, group, [mirrored[0]])
    start = direct(place, tables, tiles, start, received, chips, group, returned[:1])
    dealt = deal_halves(start, returned)
    factor, inverse = cholesky(gate(gram, dealt[0][0]))
    quarters = [reduce_half(*dealt[0], [inverse])]
    across = swap(quarters[0], "by", 3)
    quarters.append(reduce_half(*dealt[1]))
    whole = jnp.concatenate(quarters, axis=0)
    gram_0 = gram_of([jnp.dot(inverse, whole, precision=HIGHEST)])
    gram_1 = all_sum(gram_0, "by", by_all)
    gram_2 = all_sum(gram_1, "wide", core_pair)
    nearby = swap(pack([(quarters[0], *every)], [(across, *every)]), "by", 1)
    pieces = [join(place, quarters[0], across, nearby)]
    across = swap(gate(quarters[1], gram_0), "by", 3)
    nearby = swap(pack([(quarters[1], *every)], [(gate(across, gram_1), *every)]), "by", 1)
    pieces.append(join(place, quarters[1], across, nearby))
    factor, inverse_2 = cholesky(gram_chips(gram_2))
    out = final(jnp.dot(inverse_2, inverse, precision=HIGHEST), pieces)
    return (out.T, factor)


def solution(mesh):
    placed = (P(("wide", "by"), None, None), P(("wide", "by")), P(("wide", "by")), P("wide", None))
    return jax.shard_map(
        local, mesh=mesh, in_specs=placed, out_specs=(P("wide", None), P()), check_vma=False
    )
```
